32 devices in a mesh: row: 4 (over z), col: 4 (over y, core), ch: 2 (over x).
Axes of the slice: x: 2, y: 2, z: 4, core: 2. Of those that a mesh axis runs over, the one named last changes fastest.
Arguments:
- spectra: float32 [384, 128, 1024], P('ch', 'row', 'col'), may hold values from 0 to 1
- pixel_factor: float32 [64, 128, 1024], P(None, 'row', 'col'), may hold values from 0.1 to 1
- channel_factor: float32 [64, 384], P(None, 'ch'), may hold values from 0.1 to 1
- labels: int32 [128, 1024], P('row', 'col'), may hold values from 0 to 3
Outputs:
- smoothed_factor: float32 [64, 128, 1024], P(None, 'row', 'col')
- new_channel: float32 [64, 384], P(None, 'ch')
The draws below stay inside these ranges and needn't reach their ends.
All inputs are finite; a program needn't handle non-finite values.
Results may differ from the reference program's by a relative error of at most 0.000068.
Values sent between devices are 32-bit elements; how exact they have to be, the bound alone decides.
A program may use at most 64 MiB of HBM per device.

```python
import math
import jax
import jax.numpy as jnp
from jax import lax

K = 64
C = 384
SMOOTH = 3
IMG_ROWS = 128
IMG_COLS = 1024


def place_ends(values, own_key, low, top_value):
    index_at = [jax.random.randint(jax.random.fold_in(own_key, axis), (), 0, length) for axis, length in enumerate(values.shape)]
    longest = values.shape.index(max(values.shape))
    beside = index_at[:longest] + [(index_at[longest] + 1) % values.shape[longest]] + index_at[longest + 1:]
    return values.at[tuple(index_at)].set(low).at[tuple(beside)].set(top_value)


def shard_levels(own_key, dims, pieces, low, largest):
    level = 1.0
    for position, parts in pieces:
        draws = jax.random.uniform(jax.random.fold_in(jax.random.fold_in(own_key, 6), position), (parts,), jnp.float32, low / len(pieces), largest / len(pieces))
        level = level * jnp.repeat(jnp.exp(draws), dims[position] // parts).reshape((-1,) + (1,) * (len(dims) - 1 - position))
    return level


def setup_inputs(seed: int = 0) -> dict:
    streams_of = jax.random.split(jax.random.key(seed), 5)
    spectra = jnp.clip(1.0 * jax.random.uniform(streams_of[0], (C, IMG_ROWS, IMG_COLS), jnp.float32) ** shard_levels(streams_of[0], (C, IMG_ROWS, IMG_COLS), ((0, 2), (1, 4), (2, 4)), -0.2, 0.2), 0.0, 1.0)
    pixel_factor = jnp.clip(jnp.exp(math.log(1.0) - 2.3025851 * jax.random.uniform(streams_of[1], (K, IMG_ROWS, IMG_COLS), jnp.float32) ** shard_levels(streams_of[1], (K, IMG_ROWS, IMG_COLS), ((1, 4), (2, 4)), -0.2, 0.2)), 0.1, 1.0)
    channel_factor = jnp.clip(jnp.exp(math.log(1.0) - 2.3025851 * jax.random.uniform(streams_of[2], (K, C), jnp.float32) ** shard_levels(streams_of[2], (K, C), ((1, 2),), -0.2, 0.2)), 0.1, 1.0)
    labels = place_ends(jax.random.randint(streams_of[3], (IMG_ROWS, IMG_COLS), 0, 4), jax.random.fold_in(streams_of[3], 1), 0, 3).astype(jnp.int32)
    return dict(spectra=spectra, pixel_factor=pixel_factor, channel_factor=channel_factor, labels=labels)


epsilon = 1e-9


def coefficients(marked):
    center = marked[1:-1, 1:-1]
    result = []
    for neighbour in (marked[:-2, 1:-1], marked[2:, 1:-1], marked[1:-1, :-2], marked[1:-1, 2:]):
        result.append(jnp.where(neighbour == 0, 0.0, jnp.where(neighbour == center, 1.0, 0.25)).astype(jnp.float32))
    return result


def smooth_once(padded, field, weights):
    combined = field + weights[0] * padded[:, :-2, 1:-1] + weights[1] * padded[:, 2:, 1:-1]
    combined = combined + weights[2] * padded[:, 1:-1, :-2] + weights[3] * padded[:, 1:-1, 2:]
    return combined / (1.0 + weights[0] + weights[1] + weights[2] + weights[3])


def reference(spectra, pixel_factor, channel_factor, labels):
    precise = lax.Precision.HIGHEST
    contraction = (((1,), (1,)), ((), ()))
    factor_rank = pixel_factor.shape[0]
    flat_pixel = pixel_factor.reshape(factor_rank, -1)
    flat_data = spectra.reshape(spectra.shape[0], -1)
    chan_top = lax.dot_general(flat_pixel, flat_data, contraction, precision=precise, preferred_element_type=jnp.float32)
    pixel_gram = lax.dot_general(flat_pixel, flat_pixel, contraction, precision=precise, preferred_element_type=jnp.float32)
    new_channel = channel_factor * chan_top / (jnp.dot(pixel_gram, channel_factor, precision=precise, preferred_element_type=jnp.float32) + epsilon)
    pixel_top = jnp.dot(new_channel, flat_data, precision=precise, preferred_element_type=jnp.float32)
    chan_gram = lax.dot_general(new_channel, new_channel, contraction, precision=precise, preferred_element_type=jnp.float32)
    lower = jnp.dot(chan_gram, flat_pixel, precision=precise, preferred_element_type=jnp.float32)
    raised = (flat_pixel * pixel_top / (lower + epsilon)).reshape(pixel_factor.shape)
    marked = jnp.pad(labels + 1, 1)
    weights = coefficients(marked)
    field = raised
    for iteration in range(SMOOTH):
        padded = jnp.pad(field, ((0, 0), (1, 1), (1, 1)))
        field = smooth_once(padded, field, weights)
    return field, new_channel
```

```python
import functools

import jax
import jax.numpy as jnp
from jax import lax
from jax.experimental import pallas as pl
from jax.experimental.pallas import tpu as pltpu
from jax.sharding import PartitionSpec as P

SMOOTH = 3
MESH = pl.DeviceIdType.MESH
LANES = 128
SUB = 8
CHUNK = 2
EARLY = 3
BAND = 8

epsilon = 1e-09


def split(value):
    high = value.astype(jnp.bfloat16)
    low = (value - high.astype(jnp.float32)).astype(jnp.bfloat16)
    return high, low


def dot(left, right, contraction):
    return lax.dot_general(
        left, right, (contraction, ((), ())), preferred_element_type=jnp.float32
    )


def dot3(left, right, contraction):
    rows = left[0].shape[0]
    both = dot(jnp.concatenate(left, axis=0), right[0], contraction)
    return both[:rows] + both[rows:] + dot(left[0], right[1], contraction)


NT = ((1,), (1,))
NN = ((1,), (0,))


def factor_kernel(
    sizes, x_hbm, w_hbm, cf_ref, lab_ref, out_hbm, nc_out,
    xs, ws, high, low, other, gram, gram_in, gram_row, nc, part, scale, field, left, right,
    mark, mark_left, mark_right, weight, first, second, done,
    load_sem, e_send, e_recv, g_send, g_recv, z_send, z_recv, n_send, n_recv,
    t_send, t_recv, c_send, c_recv, r_send, r_recv, m_send, m_recv, out_sem,
):
    n_row, n_col, n_ch = sizes
    rank, rows, cols = w_hbm.shape
    chans = x_hbm.shape[0]
    share = rank // n_col
    early = rows - EARLY
    chunks = (early - SMOOTH) // CHUNK
    main = chunks * CHUNK
    tip = early - main
    bands = rank // BAND
    tall = rows + 2 * SMOOTH
    wide = cols + LANES
    me_row, me_col, me_ch = (lax.axis_index(a) for a in ("row", "col", "ch"))

    halves = cols // LANES
    groups = rows // SUB

    def load(g):
        start = pl.multiple_of(g * SUB, SUB)
        for h in range(halves):
            for j, (source, target) in enumerate(((w_hbm, ws), (x_hbm, xs))):
                yield pltpu.make_async_copy(
                    source.at[:, pl.ds(start, SUB), pl.ds(h * LANES, LANES)],
                    target.at[g, h],
                    load_sem.at[j, h, g],
                )

    def image_row(buffer, s):
        _, depth, _, _ = buffer.shape
        return jnp.concatenate(
            [
                buffer.at[h].reshape(depth * SUB, LANES)[pl.ds(s, depth, stride=SUB), :]
                for h in range(halves)
            ],
            axis=1,
        )

    for g in range(groups):
        for copy in load(g):
            copy.start()

    barrier = pltpu.get_barrier_semaphore()
    for d in range(1, n_row):
        pl.semaphore_signal(
            barrier, inc=1, device_id={"row": lax.rem(me_row + d, n_row)}, device_id_type=MESH
        )
    for d in range(1, n_col * n_ch):
        pl.semaphore_signal(
            barrier, inc=1, device_id=side(me_col, me_ch, d, n_col, n_ch), device_id_type=MESH
        )

    for buffer, edge in (
        (left, 0), (mark_left, 0), (right, n_col - 1), (mark_right, n_col - 1),
    ):

        @pl.when(me_col == edge)
        def _():
            buffer[...] = jnp.zeros_like(buffer)

    for at, edge in ((0, 0), (rows + SMOOTH, n_row - 1)):
        for buffer in (field, mark):

            @pl.when(me_row == edge)
            def _():
                buffer[pl.ds(at, SMOOTH)] = jnp.zeros((SMOOTH,) + buffer.shape[1:], jnp.float32)

    def marks(r, carry):
        row = (lab_ref[pl.ds(r, 1), :] + 1).astype(jnp.float32)
        mark[r + SMOOTH, :, pl.ds(0, cols)] = jnp.broadcast_to(row, (SUB, cols))
        return carry

    lax.fori_loop(0, rows, marks, 0)

    gram[...] = jnp.zeros_like(gram)

    def to_early(d, h):
        return pltpu.make_async_remote_copy(
            x_hbm.at[:, pl.ds(early, EARLY), pl.ds(h * LANES, LANES)],
            other.at[d - 1, h, :, pl.ds(SUB - EARLY, EARLY), :],
            e_send.at[d - 1, h], e_recv.at[d - 1, h],
            device_id={"ch": lax.rem(me_ch + d, n_ch)}, device_id_type=MESH,
        )

    def beside(step, source, target, at):
        return pltpu.make_async_remote_copy(
            source, target, *at, device_id={"col": lax.rem(me_col + n_col + step, n_col)},
            device_id_type=MESH,
        )

    def mark_side(step):
        k, start, target = ((0, cols - LANES, mark_left), (1, 0, mark_right))[step < 0]
        return beside(
            step, mark.at[pl.ds(SMOOTH, rows), :, pl.ds(start, LANES)], target,
            (m_send.at[k], m_recv.at[k]),
        )

    def across(step, buffer, at):
        start, end = ((rows, 0), (SMOOTH, rows + SMOOTH))[step < 0]
        return pltpu.make_async_remote_copy(
            buffer.at[pl.ds(start, SMOOTH)], buffer.at[pl.ds(end, SMOOTH)], *at,
            device_id={"row": lax.rem(me_row + n_row + step, n_row)}, device_id_type=MESH,
        )

    def mark_across(step):
        k = 2 + (step < 0)
        return across(step, mark, (m_send.at[k], m_recv.at[k]))

    def field_across(step):
        k = int(step < 0)
        return across(step, field, (r_send.at[k], r_recv.at[k]))

    def start_pair(copy, me, n):
        @pl.when(me < n - 1)
        def _():
            copy(1).start()

        @pl.when(me > 0)
        def _():
            copy(-1).start()

    def receive_pair(copy, me, n):
        @pl.when(me > 0)
        def _():
            copy(1).wait_recv()

        @pl.when(me < n - 1)
        def _():
            copy(-1).wait_recv()

    def sent_pair(copy, me, n):
        @pl.when(me < n - 1)
        def _():
            copy(1).wait_send()

        @pl.when(me > 0)
        def _():
            copy(-1).wait_send()

    pl.semaphore_wait(barrier, n_row - 1 + n_col * n_ch - 1)
    for d in range(1, n_ch):
        for h in range(halves):
            to_early(d, h).start()
    start_pair(mark_side, me_col, n_col)

    def gather(g, carry):
        for copy in load(g):
            copy.wait()
        upper = lower = 0.0
        for s in range(SUB):
            both = jnp.concatenate([image_row(ws.at[g], s), image_row(xs.at[g], s)], axis=0)
            h, l = split(both)
            high[g * SUB + s] = h
            low[g * SUB + s] = l
            upper = upper + dot(jnp.concatenate([h[:rank], l[:rank]], axis=0), h, NT)
            lower = lower + dot(h[:rank], l, NT)
        gram[...] += (upper[:rank] + upper[rank:] + lower).reshape(gram.shape)
        return carry

    lax.fori_loop(0, groups, gather, 0)

    def to_col(d):
        peer = lax.rem(me_col + d, n_col)
        return pltpu.make_async_remote_copy(
            gram.at[peer], gram_in.at[d - 1], g_send.at[d - 1], g_recv.at[d - 1],
            device_id={"col": peer}, device_id_type=MESH,
        )

    for d in range(1, n_col):
        to_col(d).start()

    lane = lax.broadcasted_iota(jnp.int32, (1, SUB, LANES), 2)

    def joined(from_left, from_right):
        return jnp.where(
            lane >= LANES - SMOOTH, from_left, jnp.where(lane < SMOOTH, from_right, 0.0)
        )

    receive_pair(mark_side, me_col, n_col)
    mark[pl.ds(SMOOTH, rows), :, pl.ds(cols, LANES)] = joined(mark_left[...], mark_right[...])
    start_pair(mark_across, me_row, n_row)

    own = gram[me_col]
    for d in range(1, n_col):
        to_col(d).wait_recv()
        own = own + gram_in[d - 1]
    gram_row[me_row] = own

    def to_row(d):
        peer = lax.rem(me_row + d, n_row)
        return pltpu.make_async_remote_copy(
            gram_row.at[me_row], gram_row.at[me_row], z_send.at[d - 1], z_recv.at[d - 1],
            device_id={"row": peer}, device_id_type=MESH,
        )

    def from_row(d):
        peer = lax.rem(me_row + n_row - d, n_row)
        return pltpu.make_async_remote_copy(
            gram_row.at[peer], gram_row.at[peer], z_send.at[d - 1], z_recv.at[d - 1],
            device_id={"row": peer}, device_id_type=MESH,
        )

    for d in range(1, n_row):
        to_row(d).start()

    receive_pair(mark_across, me_row, n_row)

    def coefficients(e, carry):
        center = mark[e]
        around = (
            mark[e - 1], mark[e + 1], pltpu.roll(center, 1, 1), pltpu.roll(center, wide - 1, 1)
        )
        parts = [
            jnp.where(near == 0, 0.0, jnp.where(near == center, 1.0, 0.25)) for near in around
        ]
        own_scale = 1.0 / (1.0 + parts[0] + parts[1] + parts[2] + parts[3])
        weight[e, 0] = own_scale
        for j in range(4):
            weight[e, j + 1] = parts[j] * own_scale
        return carry

    lax.fori_loop(1, tall - 1, coefficients, 0)

    for d in range(1, n_row):
        from_row(d).wait_recv()
    total = gram_row[0]
    for z in range(1, n_row):
        total = total + gram_row[z]
    under = jnp.dot(
        total[:, :rank], cf_ref[...], precision=lax.Precision.HIGHEST,
        preferred_element_type=jnp.float32,
    )
    own_cf = cf_ref[pl.ds(pl.multiple_of(me_col * share, share), share), :]
    nc[me_ch, me_col] = own_cf * total[:, rank:] / (under + epsilon)

    def to_side(d):
        return pltpu.make_async_remote_copy(
            nc.at[me_ch, me_col], nc.at[me_ch, me_col], n_send.at[d - 1], n_recv.at[d - 1],
            device_id=side(me_col, me_ch, d, n_col, n_ch), device_id_type=MESH,
        )

    def from_side(d):
        at = side(me_col, me_ch, n_col * n_ch - d, n_col, n_ch)
        slot = nc.at[at["ch"], at["col"]]
        return pltpu.make_async_remote_copy(
            slot, slot, n_send.at[d - 1], n_recv.at[d - 1],
            device_id=at, device_id_type=MESH,
        )

    same = [d for d in range(1, n_col * n_ch) if d % n_ch == 0]
    away = [d for d in range(1, n_col * n_ch) if d % n_ch]
    for d in same + away:
        to_side(d).start()
    for d in same:
        from_side(d).wait_recv()

    mine = nc[me_ch].reshape(rank, chans)
    nc_out[...] = mine

    def stacked(value):
        h, l = split(value)
        return jnp.concatenate([h, l], axis=0)

    mine = stacked(mine)

    def product(pair, h, l):
        depth = pair.shape[0] // 2
        both = dot(pair, h, NN)
        return both[:depth] + both[depth:] + dot(pair[:depth], l, NN)

    def own_part(r):
        at = (pl.ds(rank, chans), slice(None))
        part[me_ch, r] = product(mine, high[(r,) + at], low[(r,) + at])

    def part_copy(d, peer, slot, k):
        return pltpu.make_async_remote_copy(
            slot, slot, t_send.at[d - 1, k], t_recv.at[d - 1, k],
            device_id={"ch": peer}, device_id_type=MESH,
        )

    def chunk_slot(h, c):
        return part.at[h, pl.ds(c * CHUNK, CHUNK)]

    def band_slot(h, q):
        return part.at[h, pl.ds(main, tip), pl.ds(pl.multiple_of(q * BAND, BAND), BAND)]

    def to_ch(d, slot, i, k):
        return part_copy(d, lax.rem(me_ch + d, n_ch), slot(me_ch, i), k)

    def from_ch(d, slot, i, k):
        peer = lax.rem(me_ch + n_ch - d, n_ch)
        return part_copy(d, peer, slot(peer, i), k)

    def send_part(c, carry):
        for k in range(CHUNK):
            own_part(c * CHUNK + k)
        for d in range(1, n_ch):
            to_ch(d, chunk_slot, c, c).start()
        return carry

    lax.fori_loop(0, chunks, send_part, 0)
    for r in range(main, early):
        own_part(r)
    for q in range(bands):
        for d in range(1, n_ch):
            to_ch(d, band_slot, q, chunks + q).start()

    for d in away:
        from_side(d).wait_recv()

    def channel_gram(h):
        block = nc[h].reshape(rank, chans)
        return lax.dot_general(
            block, block, (NT, ((), ())), precision=lax.Precision.HIGHEST,
            preferred_element_type=jnp.float32,
        )

    cg = channel_gram(0)
    for h in range(1, n_ch):
        cg = cg + channel_gram(h)
    cg = stacked(cg)

    def scales(r, carry):
        g, s = r // SUB, lax.rem(r, SUB)
        below = product(cg, high[r, pl.ds(0, rank), :], low[r, pl.ds(0, rank), :])
        scale[r] = image_row(ws.at[g], s) / (below + epsilon)
        return carry

    lax.fori_loop(0, rows, scales, 0)

    for r in range(early, rows):
        own_part(r)
    for d in range(1, n_ch):
        peer = lax.rem(me_ch + n_ch - d, n_ch)
        theirs = stacked(nc[peer].reshape(rank, chans))
        for h in range(halves):
            to_early(d, h).wait_recv()
        for r in range(early, rows):
            part[peer, r] = product(theirs, *split(image_row(other.at[d - 1], r - rows + SUB)))

    every = (0, rank)

    def field_side(start, count, band, k):
        def copy(step):
            j, lanes, target = ((0, cols - LANES, left), (1, 0, right))[step < 0]
            return beside(
                step,
                field.at[pl.ds(start + SMOOTH, count), pl.ds(*band), pl.ds(lanes, LANES)],
                target.at[pl.ds(start, count), pl.ds(*band)],
                (c_send.at[j, k], c_recv.at[j, k]),
            )
        return copy

    def raise_rows(start, count, band, k):
        at = (pl.ds(start, count), pl.ds(*band))
        top = part[(0,) + at]
        for h in range(1, n_ch):
            top = top + part[(h,) + at]
        field[pl.ds(start + SMOOTH, count), pl.ds(*band), pl.ds(0, cols)] = scale[at] * top
        start_pair(field_side(start, count, band, k), me_col, n_col)

    def widen_rows(start, count, band, k):
        receive_pair(field_side(start, count, band, k), me_col, n_col)
        at = (pl.ds(start, count), pl.ds(*band))
        shape = (count * band[1] // SUB, SUB, LANES)
        edge = joined(left[at].reshape(shape), right[at].reshape(shape))
        field[pl.ds(start + SMOOTH, count), pl.ds(*band), pl.ds(cols, LANES)] = edge.reshape(
            count, band[1], LANES
        )

    def raise_chunk(c):
        for d in range(1, n_ch):
            from_ch(d, chunk_slot, c, c).wait_recv()
        raise_rows(c * CHUNK, CHUNK, every, c)

    def widen_chunk(c):
        widen_rows(c * CHUNK, CHUNK, every, c)

    def smooth(source, e, band):
        here, up, down = (
            source[at, pl.ds(*band), :].reshape(band[1] // SUB, SUB, wide)
            for at in (e, e - 1, e + 1)
        )
        total = weight[e, 0] * here + weight[e, 1] * up + weight[e, 2] * down
        total = total + weight[e, 3] * pltpu.roll(here, 1, 2)
        total = total + weight[e, 4] * pltpu.roll(here, wide - 1, 2)
        return total.reshape(band[1], wide)

    def put(r):
        return pltpu.make_async_copy(done.at[r], out_hbm.at[:, r, :], out_sem.at[r])

    def one(e, band=every):
        first[e, pl.ds(*band), :] = smooth(field, e, band)

    def two(e, band=every):
        second[e, pl.ds(*band), :] = smooth(first, e, band)

    def three(e, band=every):
        done[e - SMOOTH, pl.ds(*band), :] = smooth(second, e, band)[:, :cols]

    def three_put(e):
        three(e)
        put(e - SMOOTH).start()

    def sweep(starts, counts):
        for stage, start, count in zip((one, two, three_put), starts, counts):
            def step(k, carry, f=stage, s=start):
                f(s + k)
                return carry
            lax.fori_loop(0, count, step, 0)

    def sweep_chunk(c):
        sweep((CHUNK * c + 2, CHUNK * c + 1, CHUNK * c), (CHUNK,) * 3)

    near = -(-SMOOTH // CHUNK)
    at_end = chunks + bands
    raise_rows(early, EARLY, every, at_end)
    for c in range(near):
        raise_chunk(c)
    widen_rows(early, EARLY, every, at_end)
    for c in range(near):
        widen_chunk(c)
    start_pair(field_across, me_row, n_row)
    for c in range(near, near + 2):
        raise_chunk(c)
    receive_pair(field_across, me_row, n_row)
    edge = early + SMOOTH
    last = rows + SMOOTH
    sweep((edge + 1, edge + 2, edge + 3), (last + 1 - edge, last - 1 - edge, max(last - 3 - edge, 0)))
    seen = near * CHUNK
    sweep((1, 2, 3), (seen + 1, seen - 1, seen - 3))

    def step(c, carry):
        widen_chunk(c - 2)
        sweep_chunk(c - 2)
        raise_chunk(c)
        return carry

    lax.fori_loop(near + 2, chunks, step, 0)

    def band_of(q):
        return (pl.multiple_of(q * BAND, BAND), BAND)

    def raise_band(q):
        for d in range(1, n_ch):
            from_ch(d, band_slot, q, chunks + q).wait_recv()
        raise_rows(main, tip, band_of(q), chunks + q)

    def finish_band(q):
        band = band_of(q)
        widen_rows(main, tip, band, chunks + q)
        for e in range(main + 2, edge + 1):
            one(e, band)
        for e in range(main + 1, edge + 2):
            two(e, band)
        for e in range(main, min(edge + 3, last)):
            three(e, band)

    widen_chunk(chunks - 2)
    sweep_chunk(chunks - 2)
    for q in range(2):
        raise_band(q)
    widen_chunk(chunks - 1)
    sweep_chunk(chunks - 1)

    def band_step(q, carry):
        finish_band(q - 2)
        raise_band(q)
        return carry

    lax.fori_loop(2, bands, band_step, 0)
    for q in (bands - 2, bands - 1):
        finish_band(q)
    for e in range(main, min(edge + 3, last)):
        put(e - SMOOTH).start()

    for d in range(1, n_col):
        to_col(d).wait_send()
    for d in range(1, n_row):
        to_row(d).wait_send()
    for d in range(1, n_col * n_ch):
        to_side(d).wait_send()
    sent_pair(mark_side, me_col, n_col)
    sent_pair(mark_across, me_row, n_row)
    sent_pair(field_across, me_row, n_row)
    sent_pair(field_side(early, EARLY, every, at_end), me_col, n_col)

    def drain_chunk(c, carry):
        sent_pair(field_side(c * CHUNK, CHUNK, every, c), me_col, n_col)
        for d in range(1, n_ch):
            to_ch(d, chunk_slot, c, c).wait_send()
        return carry

    lax.fori_loop(0, chunks, drain_chunk, 0)

    def drain_band(q, carry):
        sent_pair(field_side(main, tip, band_of(q), chunks + q), me_col, n_col)
        for d in range(1, n_ch):
            to_ch(d, band_slot, q, chunks + q).wait_send()
        return carry

    lax.fori_loop(0, bands, drain_band, 0)
    for d in range(1, n_ch):
        for h in range(halves):
            to_early(d, h).wait_send()

    def drain_out(r, carry):
        put(r).wait()
        return carry

    lax.fori_loop(0, rows, drain_out, 0)


def side(me_col, me_ch, d, n_col, n_ch):
    place = lax.rem(me_col * n_ch + me_ch + d, n_col * n_ch)
    return {"col": place // n_ch, "ch": lax.rem(place, n_ch)}


def shards(sizes, spectra, pixel_factor, channel_factor, labels):
    n_row, n_col, n_ch = sizes
    rank, rows, cols = pixel_factor.shape
    chans = spectra.shape[0]
    share = rank // n_col
    early = rows - EARLY
    pieces = (early - SMOOTH) // CHUNK + rank // BAND
    tall = rows + 2 * SMOOTH
    wide = cols + LANES
    halves, groups = cols // LANES, rows // SUB
    f32 = jnp.float32
    vmem = pl.BlockSpec(memory_space=pltpu.VMEM)
    anywhere = pl.BlockSpec(memory_space=pl.ANY)
    dma = pltpu.SemaphoreType.DMA
    return pl.pallas_call(
        functools.partial(factor_kernel, sizes),
        out_shape=(
            jax.ShapeDtypeStruct(pixel_factor.shape, f32),
            jax.ShapeDtypeStruct(channel_factor.shape, f32),
        ),
        in_specs=[anywhere, anywhere, vmem, vmem],
        out_specs=(anywhere, vmem),
        scratch_shapes=[
            pltpu.VMEM((groups, halves, chans, SUB, LANES), f32),
            pltpu.VMEM((groups, halves, rank, SUB, LANES), f32),
            pltpu.VMEM((rows, rank + chans, cols), jnp.bfloat16),
            pltpu.VMEM((rows, rank + chans, cols), jnp.bfloat16),
            pltpu.VMEM((n_ch - 1, halves, chans, SUB, LANES), f32),
            pltpu.VMEM((n_col, share, rank + chans), f32),
            pltpu.VMEM((n_col - 1, share, rank + chans), f32),
            pltpu.VMEM((n_row, share, rank + chans), f32),
            pltpu.VMEM((n_ch, n_col, share, chans), f32),
            pltpu.VMEM((n_ch, rows, rank, cols), f32),
            pltpu.VMEM((rows, rank, cols), f32),
            pltpu.VMEM((tall, rank, wide), f32),
            pltpu.VMEM((rows, rank, LANES), f32),
            pltpu.VMEM((rows, rank, LANES), f32),
            pltpu.VMEM((tall, SUB, wide), f32),
            pltpu.VMEM((rows, SUB, LANES), f32),
            pltpu.VMEM((rows, SUB, LANES), f32),
            pltpu.VMEM((tall, 5, SUB, wide), f32),
            pltpu.VMEM((tall, rank, wide), f32),
            pltpu.VMEM((tall, rank, wide), f32),
            pltpu.VMEM((rows, rank, cols), f32),
            dma((2, halves, groups)),
            dma((n_ch - 1, halves)), dma((n_ch - 1, halves)),
            dma((n_col - 1,)), dma((n_col - 1,)),
            dma((n_row - 1,)), dma((n_row - 1,)),
            dma((n_col * n_ch - 1,)), dma((n_col * n_ch - 1,)),
            dma((n_ch - 1, pieces)), dma((n_ch - 1, pieces)),
            dma((2, pieces + 1)), dma((2, pieces + 1)),
            dma((2,)), dma((2,)),
            dma((4,)), dma((4,)),
            dma((rows,)),
        ],
        compiler_params=pltpu.CompilerParams(
            collective_id=0, has_side_effects=True, vmem_limit_bytes=60 * 1024 * 1024
        ),
        name="factor",
    )(spectra, pixel_factor, channel_factor, labels)


def solution(mesh):
    sizes = tuple(mesh.shape[a] for a in ("row", "col", "ch"))
    placed = (P("ch", "row", "col"), P(None, "row", "col"), P(None, "ch"), P("row", "col"))
    return jax.shard_map(
        functools.partial(shards, sizes),
        mesh=mesh,
        in_specs=placed,
        out_specs=(P(None, "row", "col"), P(None, "ch")),
        check_vma=False,
    )
```

```python
import functools

import jax
import jax.numpy as jnp
from jax import lax
from jax.experimental import pallas as pl
from jax.experimental.pallas import tpu as pltpu
from jax.sharding import PartitionSpec as P

SMOOTH = 3
MESH = pl.DeviceIdType.MESH
LANES = 128
SUB = 8
CHUNK = 2
EARLY = 3
BAND = 8
LAG = 6

epsilon = 1e-09


def split(value):
    high = value.astype(jnp.bfloat16)
    low = (value - high.astype(jnp.float32)).astype(jnp.bfloat16)
    return high, low


def dot(left, right, contraction):
    return lax.dot_general(
        left, right, (contraction, ((), ())), preferred_element_type=jnp.float32
    )


def dot3(left, right, contraction):
    rows = left[0].shape[0]
    both = dot(jnp.concatenate(left, axis=0), right[0], contraction)
    return both[:rows] + both[rows:] + dot(left[0], right[1], contraction)


NT = ((1,), (1,))
NN = ((1,), (0,))


def factor_kernel(
    sizes, x_hbm, w_hbm, cf_hbm, lab_hbm, done, nc_out,
    cf_ref, lab_ref, xs, ws, high, low, other, gram, gram_in, gram_row, nc, part, scale, field, left, right,
    mark, mark_left, mark_right, weight, first, second,
    load_sem, e_send, e_recv, g_send, g_recv, z_send, z_recv, n_send, n_recv,
    t_send, t_recv, c_send, c_recv, r_send, r_recv, m_send, m_recv, small_sem,
):
    n_row, n_col, n_ch = sizes
    rank, rows, cols = w_hbm.shape
    chans = x_hbm.shape[0]
    share = rank // n_col
    early = rows - EARLY
    chunks = (early - SMOOTH) // CHUNK
    main = chunks * CHUNK
    tip = early - main
    bands = rank // BAND
    tall = rows + 2 * SMOOTH
    wide = cols + LANES
    me_row, me_col, me_ch = (lax.axis_index(a) for a in ("row", "col", "ch"))

    halves = cols // LANES
    groups = rows // SUB

    def load(g):
        start = pl.multiple_of(g * SUB, SUB)
        for h in range(halves):
            for j, (source, target) in enumerate(((w_hbm, ws), (x_hbm, xs))):
                yield pltpu.make_async_copy(
                    source.at[:, pl.ds(start, SUB), pl.ds(h * LANES, LANES)],
                    target.at[g, h],
                    load_sem.at[j, h, g],
                )

    def image_row(buffer, s):
        _, depth, _, _ = buffer.shape
        return jnp.concatenate(
            [
                buffer.at[h].reshape(depth * SUB, LANES)[pl.ds(s, depth, stride=SUB), :]
                for h in range(halves)
            ],
            axis=1,
        )

    barrier = pltpu.get_barrier_semaphore()
    for d in range(1, n_row):
        pl.semaphore_signal(
            barrier, inc=1, device_id={"row": lax.rem(me_row + d, n_row)}, device_id_type=MESH
        )
    for d in range(1, n_col * n_ch):
        pl.semaphore_signal(
            barrier, inc=1, device_id=side(me_col, me_ch, d, n_col, n_ch), device_id_type=MESH
        )

    def to_early(d, h):
        return pltpu.make_async_remote_copy(
            x_hbm.at[:, pl.ds(early, EARLY), pl.ds(h * LANES, LANES)],
            other.at[d - 1, h, :, pl.ds(SUB - EARLY, EARLY), :],
            e_send.at[d - 1, h], e_recv.at[d - 1, h],
            device_id={"ch": lax.rem(me_ch + d, n_ch)}, device_id_type=MESH,
        )

    def beside(step, source, target, at):
        return pltpu.make_async_remote_copy(
            source, target, *at, device_id={"col": lax.rem(me_col + n_col + step, n_col)},
            device_id_type=MESH,
        )

    def mark_side(step):
        k, start, target = ((0, cols - LANES, mark_left), (1, 0, mark_right))[step < 0]
        return beside(
            step, mark.at[pl.ds(SMOOTH, rows), :, pl.ds(start, LANES)], target,
            (m_send.at[k], m_recv.at[k]),
        )

    def across(step, buffer, at):
        start, end = ((rows, 0), (SMOOTH, rows + SMOOTH))[step < 0]
        return pltpu.make_async_remote_copy(
            buffer.at[pl.ds(start, SMOOTH)], buffer.at[pl.ds(end, SMOOTH)], *at,
            device_id={"row": lax.rem(me_row + n_row + step, n_row)}, device_id_type=MESH,
        )

    def mark_across(step):
        k = 2 + (step < 0)
        return across(step, mark, (m_send.at[k], m_recv.at[k]))

    def field_across(step):
        k = int(step < 0)
        return across(step, field, (r_send.at[k], r_recv.at[k]))

    def start_pair(copy, me, n):
        @pl.when(me < n - 1)
        def _():
            copy(1).start()

        @pl.when(me > 0)
        def _():
            copy(-1).start()

    def receive_pair(copy, me, n):
        @pl.when(me > 0)
        def _():
            copy(1).wait_recv()

        @pl.when(me < n - 1)
        def _():
            copy(-1).wait_recv()

    def sent_pair(copy, me, n):
        @pl.when(me < n - 1)
        def _():
            copy(1).wait_send()

        @pl.when(me > 0)
        def _():
            copy(-1).wait_send()

    for copy in load(0):
        copy.start()
    lab_load = pltpu.make_async_copy(lab_hbm, lab_ref, small_sem.at[0])
    cf_load = pltpu.make_async_copy(cf_hbm, cf_ref, small_sem.at[1])
    lab_load.start()
    pl.semaphore_wait(barrier, n_row - 1 + n_col * n_ch - 1)
    for d in range(1, n_ch):
        for h in range(halves):
            to_early(d, h).start()
    for g in range(1, groups):
        for copy in load(g):
            copy.start()
    cf_load.start()

    for buffer, edge in (
        (left, 0), (mark_left, 0), (right, n_col - 1), (mark_right, n_col - 1),
    ):

        @pl.when(me_col == edge)
        def _():
            buffer[...] = jnp.zeros_like(buffer)

    for at, edge in ((0, 0), (rows + SMOOTH, n_row - 1)):
        for buffer in (field, mark):

            @pl.when(me_row == edge)
            def _():
                buffer[pl.ds(at, SMOOTH)] = jnp.zeros((SMOOTH,) + buffer.shape[1:], jnp.float32)

    lab_load.wait()

    def marks(r, carry):
        row = (lab_ref[pl.ds(r, 1), :] + 1).astype(jnp.float32)
        mark[r + SMOOTH, :, pl.ds(0, cols)] = jnp.broadcast_to(row, (SUB, cols))
        return carry

    lax.fori_loop(0, rows, marks, 0)

    gram[...] = jnp.zeros_like(gram)

    start_pair(mark_side, me_col, n_col)

    def gather(g, carry):
        for copy in load(g):
            copy.wait()
        upper = lower = 0.0
        for s in range(SUB):
            both = jnp.concatenate([image_row(ws.at[g], s), image_row(xs.at[g], s)], axis=0)
            h, l = split(both)
            high[g * SUB + s] = h
            low[g * SUB + s] = l
            upper = upper + dot(jnp.concatenate([h[:rank], l[:rank]], axis=0), h, NT)
            lower = lower + dot(h[:rank], l, NT)
        gram[...] += (upper[:rank] + upper[rank:] + lower).reshape(gram.shape)
        return carry

    lax.fori_loop(0, groups, gather, 0)

    def to_col(d):
        peer = lax.rem(me_col + d, n_col)
        return pltpu.make_async_remote_copy(
            gram.at[peer], gram_in.at[d - 1], g_send.at[d - 1], g_recv.at[d - 1],
            device_id={"col": peer}, device_id_type=MESH,
        )

    for d in range(1, n_col):
        to_col(d).start()

    lane = lax.broadcasted_iota(jnp.int32, (1, SUB, LANES), 2)

    def joined(from_left, from_right):
        return jnp.where(
            lane >= LANES - SMOOTH, from_left, jnp.where(lane < SMOOTH, from_right, 0.0)
        )

    receive_pair(mark_side, me_col, n_col)
    mark[pl.ds(SMOOTH, rows), :, pl.ds(cols, LANES)] = joined(mark_left[...], mark_right[...])
    start_pair(mark_across, me_row, n_row)

    own = gram[me_col]
    for d in range(1, n_col):
        to_col(d).wait_recv()
        own = own + gram_in[d - 1]
    gram_row[me_row] = own

    def to_row(d):
        peer = lax.rem(me_row + d, n_row)
        return pltpu.make_async_remote_copy(
            gram_row.at[me_row], gram_row.at[me_row], z_send.at[d - 1], z_recv.at[d - 1],
            device_id={"row": peer}, device_id_type=MESH,
        )

    def from_row(d):
        peer = lax.rem(me_row + n_row - d, n_row)
        return pltpu.make_async_remote_copy(
            gram_row.at[peer], gram_row.at[peer], z_send.at[d - 1], z_recv.at[d - 1],
            device_id={"row": peer}, device_id_type=MESH,
        )

    for d in range(1, n_row):
        to_row(d).start()

    receive_pair(mark_across, me_row, n_row)

    def coefficients(e, carry):
        center = mark[e]
        around = (
            mark[e - 1], mark[e + 1], pltpu.roll(center, 1, 1), pltpu.roll(center, wide - 1, 1)
        )
        parts = [
            jnp.where(near == 0, 0.0, jnp.where(near == center, 1.0, 0.25)) for near in around
        ]
        own_scale = 1.0 / (1.0 + parts[0] + parts[1] + parts[2] + parts[3])
        weight[e, 0] = own_scale
        for j in range(4):
            weight[e, j + 1] = parts[j] * own_scale
        return carry

    lax.fori_loop(1, tall - 1, coefficients, 0)
    cf_load.wait()

    for d in range(1, n_row):
        from_row(d).wait_recv()
    total = gram_row[0]
    for z in range(1, n_row):
        total = total + gram_row[z]
    under = jnp.dot(
        total[:, :rank], cf_ref[...], precision=lax.Precision.HIGHEST,
        preferred_element_type=jnp.float32,
    )
    own_cf = cf_ref[pl.ds(pl.multiple_of(me_col * share, share), share), :]
    nc[me_ch, me_col] = own_cf * total[:, rank:] / (under + epsilon)

    def to_side(d):
        return pltpu.make_async_remote_copy(
            nc.at[me_ch, me_col], nc.at[me_ch, me_col], n_send.at[d - 1], n_recv.at[d - 1],
            device_id=side(me_col, me_ch, d, n_col, n_ch), device_id_type=MESH,
        )

    def from_side(d):
        at = side(me_col, me_ch, n_col * n_ch - d, n_col, n_ch)
        slot = nc.at[at["ch"], at["col"]]
        return pltpu.make_async_remote_copy(
            slot, slot, n_send.at[d - 1], n_recv.at[d - 1],
            device_id=at, device_id_type=MESH,
        )

    same = [d for d in range(1, n_col * n_ch) if d % n_ch == 0]
    away = [d for d in range(1, n_col * n_ch) if d % n_ch]
    for d in same + away:
        to_side(d).start()
    for d in same:
        from_side(d).wait_recv()

    mine = nc[me_ch].reshape(rank, chans)
    nc_out[...] = mine

    def stacked(value):
        h, l = split(value)
        return jnp.concatenate([h, l], axis=0)

    mine = stacked(mine)

    def product(pair, h, l):
        depth = pair.shape[0] // 2
        both = dot(pair, h, NN)
        return both[:depth] + both[depth:] + dot(pair[:depth], l, NN)

    def own_part(r):
        at = (pl.ds(rank, chans), slice(None))
        part[me_ch, r] = product(mine, high[(r,) + at], low[(r,) + at])

    def part_copy(d, peer, slot, k):
        return pltpu.make_async_remote_copy(
            slot, slot, t_send.at[d - 1, k], t_recv.at[d - 1, k],
            device_id={"ch": peer}, device_id_type=MESH,
        )

    def chunk_slot(h, c):
        return part.at[h, pl.ds(c * CHUNK, CHUNK)]

    def band_slot(h, q):
        return part.at[h, pl.ds(main, tip), pl.ds(pl.multiple_of(q * BAND, BAND), BAND)]

    def to_ch(d, slot, i, k):
        return part_copy(d, lax.rem(me_ch + d, n_ch), slot(me_ch, i), k)

    def from_ch(d, slot, i, k):
        peer = lax.rem(me_ch + n_ch - d, n_ch)
        return part_copy(d, peer, slot(peer, i), k)

    def send_part(c, carry):
        for k in range(CHUNK):
            own_part(c * CHUNK + k)
        for d in range(1, n_ch):
            to_ch(d, chunk_slot, c, c).start()
        return carry

    lax.fori_loop(0, chunks, send_part, 0)
    for r in range(main, early):
        own_part(r)
    for q in range(bands):
        for d in range(1, n_ch):
            to_ch(d, band_slot, q, chunks + q).start()

    for d in away:
        from_side(d).wait_recv()

    def channel_gram(h):
        block = nc[h].reshape(rank, chans)
        return lax.dot_general(
            block, block, (NT, ((), ())), precision=lax.Precision.HIGHEST,
            preferred_element_type=jnp.float32,
        )

    cg = channel_gram(0)
    for h in range(1, n_ch):
        cg = cg + channel_gram(h)
    cg = stacked(cg)

    def scales(r, carry):
        g, s = r // SUB, lax.rem(r, SUB)
        below = product(cg, high[r, pl.ds(0, rank), :], low[r, pl.ds(0, rank), :])
        scale[r] = image_row(ws.at[g], s) / (below + epsilon)
        return carry

    lax.fori_loop(0, rows, scales, 0)

    for r in range(early, rows):
        own_part(r)
    for d in range(1, n_ch):
        peer = lax.rem(me_ch + n_ch - d, n_ch)
        theirs = stacked(nc[peer].reshape(rank, chans))
        for h in range(halves):
            to_early(d, h).wait_recv()
        for r in range(early, rows):
            part[peer, r] = product(theirs, *split(image_row(other.at[d - 1], r - rows + SUB)))

    every = (0, rank)

    def field_side(start, count, band, k):
        def copy(step):
            j, lanes, target = ((0, cols - LANES, left), (1, 0, right))[step < 0]
            return beside(
                step,
                field.at[pl.ds(start + SMOOTH, count), pl.ds(*band), pl.ds(lanes, LANES)],
                target.at[pl.ds(start, count), pl.ds(*band)],
                (c_send.at[j, k], c_recv.at[j, k]),
            )
        return copy

    def raise_rows(start, count, band, k):
        at = (pl.ds(start, count), pl.ds(*band))
        top = part[(0,) + at]
        for h in range(1, n_ch):
            top = top + part[(h,) + at]
        field[pl.ds(start + SMOOTH, count), pl.ds(*band), pl.ds(0, cols)] = scale[at] * top
        start_pair(field_side(start, count, band, k), me_col, n_col)

    def widen_rows(start, count, band, k):
        receive_pair(field_side(start, count, band, k), me_col, n_col)
        at = (pl.ds(start, count), pl.ds(*band))
        shape = (count * band[1] // SUB, SUB, LANES)
        edge = joined(left[at].reshape(shape), right[at].reshape(shape))
        field[pl.ds(start + SMOOTH, count), pl.ds(*band), pl.ds(cols, LANES)] = edge.reshape(
            count, band[1], LANES
        )

    def raise_chunk(c):
        for d in range(1, n_ch):
            from_ch(d, chunk_slot, c, c).wait_recv()
        raise_rows(c * CHUNK, CHUNK, every, c)

    def widen_chunk(c):
        widen_rows(c * CHUNK, CHUNK, every, c)

    def smooth(source, e, band):
        here, up, down = (
            source[at, pl.ds(*band), :].reshape(band[1] // SUB, SUB, wide)
            for at in (e, e - 1, e + 1)
        )
        total = weight[e, 0] * here + weight[e, 1] * up + weight[e, 2] * down
        total = total + weight[e, 3] * pltpu.roll(here, 1, 2)
        total = total + weight[e, 4] * pltpu.roll(here, wide - 1, 2)
        return total.reshape(band[1], wide)

    def one(e, band=every):
        first[e, pl.ds(*band), :] = smooth(field, e, band)

    def two(e, band=every):
        second[e, pl.ds(*band), :] = smooth(first, e, band)

    def three(e, band=every):
        value = smooth(second, e, band)
        for h in range(halves):
            rows_of = done.at[h].reshape(rank * rows, LANES)
            start = band[0] * rows + e - SMOOTH
            rows_of[pl.ds(start, band[1], stride=rows), :] = value[:, h * LANES:(h + 1) * LANES]

    def sweep(starts, counts):
        for stage, start, count in zip((one, two, three), starts, counts):
            def step(k, carry, f=stage, s=start):
                f(s + k)
                return carry
            lax.fori_loop(0, count, step, 0)

    def sweep_chunk(c):
        sweep((CHUNK * c + 2, CHUNK * c + 1, CHUNK * c), (CHUNK,) * 3)

    near = -(-SMOOTH // CHUNK)
    at_end = chunks + bands
    raise_rows(early, EARLY, every, at_end)
    for c in range(near):
        raise_chunk(c)
    widen_rows(early, EARLY, every, at_end)
    for c in range(near):
        widen_chunk(c)
    start_pair(field_across, me_row, n_row)
    for c in range(near, near + 2):
        raise_chunk(c)
    receive_pair(field_across, me_row, n_row)
    edge = early + SMOOTH
    last = rows + SMOOTH
    sweep((edge + 1, edge + 2, edge + 3), (last + 1 - edge, last - 1 - edge, max(last - 3 - edge, 0)))
    seen = near * CHUNK
    sweep((1, 2, 3), (seen + 1, seen - 1, seen - 3))

    def step(c, carry):
        widen_chunk(c - 2)
        sweep_chunk(c - 2)
        raise_chunk(c)
        return carry

    lax.fori_loop(near + 2, chunks, step, 0)

    def band_of(q):
        return (pl.multiple_of(q * BAND, BAND), BAND)

    def raise_band(q):
        for d in range(1, n_ch):
            from_ch(d, band_slot, q, chunks + q).wait_recv()
        raise_rows(main, tip, band_of(q), chunks + q)

    def finish_band(q):
        band = band_of(q)
        widen_rows(main, tip, band, chunks + q)
        for e in range(main + 2, edge + 1):
            one(e, band)
        for e in range(main + 1, edge + 2):
            two(e, band)
        for e in range(main, min(edge + 3, last)):
            three(e, band)

    widen_chunk(chunks - 2)
    sweep_chunk(chunks - 2)
    for q in range(2):
        raise_band(q)
    widen_chunk(chunks - 1)
    sweep_chunk(chunks - 1)

    def rise(q, carry):
        raise_band(q)
        return carry

    def rise_and_finish(q, carry):
        raise_band(q)
        finish_band(q - LAG)
        return carry

    def finish(q, carry):
        finish_band(q)
        return carry

    lax.fori_loop(2, LAG, rise, 0)
    lax.fori_loop(LAG, bands, rise_and_finish, 0)
    lax.fori_loop(bands - LAG, bands, finish, 0)

    for d in range(1, n_col):
        to_col(d).wait_send()
    for d in range(1, n_row):
        to_row(d).wait_send()
    for d in range(1, n_col * n_ch):
        to_side(d).wait_send()
    sent_pair(mark_side, me_col, n_col)
    sent_pair(mark_across, me_row, n_row)
    sent_pair(field_across, me_row, n_row)
    sent_pair(field_side(early, EARLY, every, at_end), me_col, n_col)

    def drain_chunk(c, carry):
        sent_pair(field_side(c * CHUNK, CHUNK, every, c), me_col, n_col)
        for d in range(1, n_ch):
            to_ch(d, chunk_slot, c, c).wait_send()
        return carry

    lax.fori_loop(0, chunks, drain_chunk, 0)

    def drain_band(q, carry):
        sent_pair(field_side(main, tip, band_of(q), chunks + q), me_col, n_col)
        for d in range(1, n_ch):
            to_ch(d, band_slot, q, chunks + q).wait_send()
        return carry

    lax.fori_loop(0, bands, drain_band, 0)
    for d in range(1, n_ch):
        for h in range(halves):
            to_early(d, h).wait_send()


def store_kernel(done, new_channel, out_hbm, nc_hbm, sem):
    copies = [pltpu.make_async_copy(new_channel, nc_hbm, sem.at[0])]
    for h in range(done.shape[0]):
        target = out_hbm.at[:, :, pl.ds(h * LANES, LANES)]
        copies.append(pltpu.make_async_copy(done.at[h], target, sem.at[h + 1]))
    for copy in copies:
        copy.start()
    for copy in copies:
        copy.wait()


def side(me_col, me_ch, d, n_col, n_ch):
    place = lax.rem(me_col * n_ch + me_ch + d, n_col * n_ch)
    return {"col": place // n_ch, "ch": lax.rem(place, n_ch)}


def shards(sizes, spectra, pixel_factor, channel_factor, labels):
    n_row, n_col, n_ch = sizes
    rank, rows, cols = pixel_factor.shape
    chans = spectra.shape[0]
    share = rank // n_col
    early = rows - EARLY
    pieces = (early - SMOOTH) // CHUNK + rank // BAND
    tall = rows + 2 * SMOOTH
    wide = cols + LANES
    halves, groups = cols // LANES, rows // SUB
    f32 = jnp.float32
    anywhere = pl.BlockSpec(memory_space=pl.ANY)
    dma = pltpu.SemaphoreType.DMA
    kept = pl.BlockSpec(memory_space=pltpu.VMEM)
    done, new_channel = pl.pallas_call(
        functools.partial(factor_kernel, sizes),
        out_shape=(
            pltpu.VMEM((halves, rank, rows, LANES), f32),
            pltpu.VMEM(channel_factor.shape, f32),
        ),
        in_specs=[anywhere] * 4,
        out_specs=(kept, kept),
        scratch_shapes=[
            pltpu.VMEM(channel_factor.shape, f32),
            pltpu.VMEM(labels.shape, labels.dtype),
            pltpu.VMEM((groups, halves, chans, SUB, LANES), f32),
            pltpu.VMEM((groups, halves, rank, SUB, LANES), f32),
            pltpu.VMEM((rows, rank + chans, cols), jnp.bfloat16),
            pltpu.VMEM((rows, rank + chans, cols), jnp.bfloat16),
            pltpu.VMEM((n_ch - 1, halves, chans, SUB, LANES), f32),
            pltpu.VMEM((n_col, share, rank + chans), f32),
            pltpu.VMEM((n_col - 1, share, rank + chans), f32),
            pltpu.VMEM((n_row, share, rank + chans), f32),
            pltpu.VMEM((n_ch, n_col, share, chans), f32),
            pltpu.VMEM((n_ch, rows, rank, cols), f32),
            pltpu.VMEM((rows, rank, cols), f32),
            pltpu.VMEM((tall, rank, wide), f32),
            pltpu.VMEM((rows, rank, LANES), f32),
            pltpu.VMEM((rows, rank, LANES), f32),
            pltpu.VMEM((tall, SUB, wide), f32),
            pltpu.VMEM((rows, SUB, LANES), f32),
            pltpu.VMEM((rows, SUB, LANES), f32),
            pltpu.VMEM((tall, 5, SUB, wide), f32),
            pltpu.VMEM((tall, rank, wide), f32),
            pltpu.VMEM((tall, rank, wide), f32),
            dma((2, halves, groups)),
            dma((n_ch - 1, halves)), dma((n_ch - 1, halves)),
            dma((n_col - 1,)), dma((n_col - 1,)),
            dma((n_row - 1,)), dma((n_row - 1,)),
            dma((n_col * n_ch - 1,)), dma((n_col * n_ch - 1,)),
            dma((n_ch - 1, pieces)), dma((n_ch - 1, pieces)),
            dma((2, pieces + 1)), dma((2, pieces + 1)),
            dma((2,)), dma((2,)),
            dma((4,)), dma((4,)),
            dma((2,)),
        ],
        compiler_params=pltpu.CompilerParams(
            collective_id=0, has_side_effects=True, vmem_limit_bytes=52 * 1024 * 1024
        ),
        name="factor",
    )(spectra, pixel_factor, channel_factor, labels)
    return pl.pallas_call(
        store_kernel,
        out_shape=(
            jax.ShapeDtypeStruct(pixel_factor.shape, f32),
            jax.ShapeDtypeStruct(channel_factor.shape, f32),
        ),
        in_specs=[kept, kept],
        out_specs=(anywhere, anywhere),
        scratch_shapes=[dma((halves + 1,))],
        compiler_params=pltpu.CompilerParams(vmem_limit_bytes=4 * 1024 * 1024),
        name="store",
    )(done, new_channel)


def solution(mesh):
    sizes = tuple(mesh.shape[a] for a in ("row", "col", "ch"))
    placed = (P("ch", "row", "col"), P(None, "row", "col"), P(None, "ch"), P("row", "col"))
    return jax.shard_map(
        functools.partial(shards, sizes),
        mesh=mesh,
        in_specs=placed,
        out_specs=(P(None, "row", "col"), P(None, "ch")),
        check_vma=False,
    )
```

```python
import functools

import jax
import jax.numpy as jnp
from jax import lax
from jax.experimental import pallas as pl
from jax.experimental.pallas import tpu as pltpu
from jax.sharding import PartitionSpec as P

SMOOTH = 3
MESH = pl.DeviceIdType.MESH
LANES = 128
SUB = 8
CHUNK = 2
EARLY = 3
BAND = 32

epsilon = 1e-09


def split(value):
    high = value.astype(jnp.bfloat16)
    low = (value - high.astype(jnp.float32)).astype(jnp.bfloat16)
    return high, low


def dot(left, right, contraction):
    return lax.dot_general(
        left, right, (contraction, ((), ())), preferred_element_type=jnp.float32
    )


def dot3(left, right, contraction):
    rows = left[0].shape[0]
    both = dot(jnp.concatenate(left, axis=0), right[0], contraction)
    return both[:rows] + both[rows:] + dot(left[0], right[1], contraction)


NT = ((1,), (1,))
NN = ((1,), (0,))


def each(start, count, width, act):
    def body(i, carry):
        for k in range(width):
            act(start + i * width + k)
        return carry

    whole = count // width
    if whole == 1:
        body(0, 0)
    elif whole:
        lax.fori_loop(0, whole, body, 0)
    for k in range(whole * width, count):
        act(start + k)


def factor_kernel(
    sizes, x_hbm, w_hbm, cf_hbm, lab_hbm, done, nc_out,
    cf_ref, lab_ref, xs, ws, high, low, other, gram, gram_in, gram_row, nc, part, scale, field, sides,
    mark, mark_left, mark_right, weight, first, second,
    load_sem, e_send, e_recv, g_send, g_recv, z_send, z_recv, n_send, n_recv,
    t_send, t_recv, c_send, c_recv, r_send, r_recv, m_send, m_recv, small_sem,
):
    n_row, n_col, n_ch = sizes
    rank, rows, cols = w_hbm.shape
    chans = x_hbm.shape[0]
    share = rank // n_col
    early = rows - EARLY
    chunks = (early - SMOOTH) // CHUNK
    main = chunks * CHUNK
    tip = early - main
    bands = rank // BAND
    tall = rows + 2 * SMOOTH
    wide = cols + LANES
    me_row, me_col, me_ch = (lax.axis_index(a) for a in ("row", "col", "ch"))

    halves = cols // LANES
    groups = rows // SUB

    def load(g):
        start = pl.multiple_of(g * SUB, SUB)
        for h in range(halves):
            for j, (source, target) in enumerate(((w_hbm, ws), (x_hbm, xs))):
                yield pltpu.make_async_copy(
                    source.at[:, pl.ds(start, SUB), pl.ds(h * LANES, LANES)],
                    target.at[g, h],
                    load_sem.at[j, h, g],
                )

    def image_row(buffer, s):
        _, depth, _, _ = buffer.shape
        return jnp.concatenate(
            [
                buffer.at[h].reshape(depth * SUB, LANES)[pl.ds(s, depth, stride=SUB), :]
                for h in range(halves)
            ],
            axis=1,
        )

    barrier = pltpu.get_barrier_semaphore()
    for d in range(1, n_row):
        pl.semaphore_signal(
            barrier, inc=1, device_id={"row": lax.rem(me_row + d, n_row)}, device_id_type=MESH
        )
    for d in range(1, n_col):
        pl.semaphore_signal(
            barrier, inc=1, device_id={"col": lax.rem(me_col + d, n_col)}, device_id_type=MESH
        )
    for d in range(1, n_ch):
        pl.semaphore_signal(
            barrier, inc=1, device_id={"ch": lax.rem(me_ch + d, n_ch)}, device_id_type=MESH
        )

    def to_early(d, h):
        return pltpu.make_async_remote_copy(
            x_hbm.at[:, pl.ds(early, EARLY), pl.ds(h * LANES, LANES)],
            other.at[d - 1, h, :, pl.ds(SUB - EARLY, EARLY), :],
            e_send.at[d - 1, h], e_recv.at[d - 1, h],
            device_id={"ch": lax.rem(me_ch + d, n_ch)}, device_id_type=MESH,
        )

    def beside(step, source, target, at):
        return pltpu.make_async_remote_copy(
            source, target, *at, device_id={"col": lax.rem(me_col + n_col + step, n_col)},
            device_id_type=MESH,
        )

    def mark_side(step):
        k, start, target = ((0, cols - LANES, mark_left), (1, 0, mark_right))[step < 0]
        return beside(
            step, mark.at[pl.ds(SMOOTH, rows), :, pl.ds(start, LANES)], target,
            (m_send.at[k], m_recv.at[k]),
        )

    def across(step, buffer, at):
        start, end = ((rows, 0), (SMOOTH, rows + SMOOTH))[step < 0]
        return pltpu.make_async_remote_copy(
            buffer.at[pl.ds(start, SMOOTH)], buffer.at[pl.ds(end, SMOOTH)], *at,
            device_id={"row": lax.rem(me_row + n_row + step, n_row)}, device_id_type=MESH,
        )

    def mark_across(step):
        k = 2 + (step < 0)
        return across(step, mark, (m_send.at[k], m_recv.at[k]))

    def field_across(step):
        k = int(step < 0)
        return across(step, field, (r_send.at[k], r_recv.at[k]))

    def start_pair(copy, me, n):
        @pl.when(me < n - 1)
        def _():
            copy(1).start()

        @pl.when(me > 0)
        def _():
            copy(-1).start()

    def receive_pair(copy, me, n):
        @pl.when(me > 0)
        def _():
            copy(1).wait_recv()

        @pl.when(me < n - 1)
        def _():
            copy(-1).wait_recv()

    def sent_pair(copy, me, n):
        @pl.when(me < n - 1)
        def _():
            copy(1).wait_send()

        @pl.when(me > 0)
        def _():
            copy(-1).wait_send()

    for copy in (*load(0), *load(1)):
        copy.start()
    lab_load = pltpu.make_async_copy(lab_hbm, lab_ref, small_sem.at[0])
    cf_load = pltpu.make_async_copy(cf_hbm, cf_ref, small_sem.at[1])
    lab_load.start()
    cf_load.start()
    pl.semaphore_wait(barrier, n_row + n_col + n_ch - 3)
    for d in range(1, n_ch):
        for h in range(halves):
            to_early(d, h).start()
    for g in range(2, groups):
        for copy in load(g):
            copy.start()

    for buffer, edge in (
        (sides.at[0], 0), (mark_left, 0), (sides.at[1], n_col - 1), (mark_right, n_col - 1),
    ):

        @pl.when(me_col == edge)
        def _():
            buffer[...] = jnp.zeros(buffer.shape, jnp.float32)

    for at, edge in ((0, 0), (rows + SMOOTH, n_row - 1)):
        for buffer in (field, mark):

            @pl.when(me_row == edge)
            def _():
                buffer[pl.ds(at, SMOOTH)] = jnp.zeros((SMOOTH,) + buffer.shape[1:], jnp.float32)

    lab_load.wait()

    def marks(r):
        row = (lab_ref[pl.ds(r, 1), :] + 1).astype(jnp.float32)
        mark[r + SMOOTH, :, pl.ds(0, cols)] = jnp.broadcast_to(row, (SUB, cols))

    each(0, rows, 8, marks)

    gram[...] = jnp.zeros_like(gram)

    start_pair(mark_side, me_col, n_col)

    def gather(g, carry):
        for copy in load(g):
            copy.wait()
        upper = lower = 0.0
        for s in range(SUB):
            both = jnp.concatenate([image_row(ws.at[g], s), image_row(xs.at[g], s)], axis=0)
            h, l = split(both)
            high[g * SUB + s] = h
            low[g * SUB + s] = l
            upper = upper + dot(jnp.concatenate([h[:rank], l[:rank]], axis=0), h, NT)
            lower = lower + dot(h[:rank], l, NT)
        gram[...] += (upper[:rank] + upper[rank:] + lower).reshape(gram.shape)
        return carry

    lax.fori_loop(0, groups, gather, 0)

    def to_col(d):
        peer = lax.rem(me_col + d, n_col)
        return pltpu.make_async_remote_copy(
            gram.at[peer], gram_in.at[d - 1], g_send.at[0], g_recv.at[d - 1],
            device_id={"col": peer}, device_id_type=MESH,
        )

    for d in range(1, n_col):
        to_col(d).start()

    lane = lax.broadcasted_iota(jnp.int32, (1, SUB, LANES), 2)

    def joined(from_left, from_right):
        return jnp.where(
            lane >= LANES - SMOOTH, from_left, jnp.where(lane < SMOOTH, from_right, 0.0)
        )

    receive_pair(mark_side, me_col, n_col)
    mark[pl.ds(SMOOTH, rows), :, pl.ds(cols, LANES)] = joined(mark_left[...], mark_right[...])
    start_pair(mark_across, me_row, n_row)

    own = gram[me_col]
    for d in range(1, n_col):
        to_col(d).wait_recv()
        own = own + gram_in[d - 1]
    gram_row[me_row] = own

    def to_row(d):
        peer = lax.rem(me_row + d, n_row)
        return pltpu.make_async_remote_copy(
            gram_row.at[me_row], gram_row.at[me_row], z_send.at[0], z_recv.at[d - 1],
            device_id={"row": peer}, device_id_type=MESH,
        )

    def from_row(d):
        peer = lax.rem(me_row + n_row - d, n_row)
        return pltpu.make_async_remote_copy(
            gram_row.at[peer], gram_row.at[peer], z_send.at[0], z_recv.at[d - 1],
            device_id={"row": peer}, device_id_type=MESH,
        )

    for d in range(1, n_row):
        to_row(d).start()

    receive_pair(mark_across, me_row, n_row)

    def coefficients(e):
        center = mark[e]
        around = (
            mark[e - 1], mark[e + 1], pltpu.roll(center, 1, 1), pltpu.roll(center, wide - 1, 1)
        )
        parts = [
            jnp.where(near == 0, 0.0, jnp.where(near == center, 1.0, 0.25)) for near in around
        ]
        own_scale = 1.0 / (1.0 + parts[0] + parts[1] + parts[2] + parts[3])
        weight[e, 0] = own_scale
        for j in range(4):
            weight[e, j + 1] = parts[j] * own_scale

    each(1, tall - 2, 4, coefficients)
    cf_load.wait()

    for d in range(1, n_row):
        from_row(d).wait_recv()
    total = gram_row[0]
    for z in range(1, n_row):
        total = total + gram_row[z]
    under = jnp.dot(
        total[:, :rank], cf_ref[...], precision=lax.Precision.HIGHEST,
        preferred_element_type=jnp.float32,
    )
    own_cf = cf_ref[pl.ds(pl.multiple_of(me_col * share, share), share), :]
    nc[me_ch, me_col] = own_cf * total[:, rank:] / (under + epsilon)

    def spread(d, back, h, k):
        col = lax.rem(me_col + (n_col - d if back else 0), n_col)
        slot = nc.at[h, col]
        return pltpu.make_async_remote_copy(
            slot, slot, n_send.at[k], n_recv.at[k],
            device_id={"col": lax.rem(me_col + d, n_col)}, device_id_type=MESH,
        )

    def cross(d, back):
        slot = nc.at[lax.rem(me_ch + (n_ch - d if back else 0), n_ch), me_col]
        k = n_col - 1 + d - 1
        return pltpu.make_async_remote_copy(
            slot, slot, n_send.at[k], n_recv.at[k],
            device_id={"ch": lax.rem(me_ch + d, n_ch)}, device_id_type=MESH,
        )

    def pass_on(d, c, back):
        k = n_col - 1 + n_ch - 1 + (d - 1) * (n_col - 1) + c - 1
        return spread(c, back, lax.rem(me_ch + n_ch - d, n_ch), k)

    for c in range(1, n_col):
        spread(c, False, me_ch, c - 1).start()
    for d in range(1, n_ch):
        cross(d, False).start()
    for c in range(1, n_col):
        spread(c, True, me_ch, c - 1).wait_recv()

    mine = nc[me_ch].reshape(rank, chans)
    nc_out[...] = mine

    def stacked(value):
        h, l = split(value)
        return jnp.concatenate([h, l], axis=0)

    mine = stacked(mine)

    def product(pair, h, l):
        depth = pair.shape[0] // 2
        both = dot(pair, h, NN)
        return both[:depth] + both[depth:] + dot(pair[:depth], l, NN)

    def own_part(r):
        at = (pl.ds(rank, chans), slice(None))
        part[me_ch, r] = product(mine, high[(r,) + at], low[(r,) + at])

    def part_copy(d, peer, slot, k):
        return pltpu.make_async_remote_copy(
            slot, slot, t_send.at[d - 1], t_recv.at[d - 1, k],
            device_id={"ch": peer}, device_id_type=MESH,
        )

    def chunk_slot(h, c):
        return part.at[h, pl.ds(c * CHUNK, CHUNK)]

    odd = lax.rem(me_col, 2)

    def lanes_of(phase):
        if phase == 0:
            return pl.ds(pl.multiple_of(odd * (cols - LANES), LANES), LANES)
        return pl.ds(pl.multiple_of((1 - odd) * LANES, LANES), cols - LANES)

    def piece_slot(phase):
        def slot(h, q):
            band = pl.ds(pl.multiple_of(q * BAND, BAND), BAND)
            return part.at[h, pl.ds(main, tip), band, lanes_of(phase)]
        return slot

    def piece(phase, q):
        return chunks + phase * bands + q

    def to_ch(d, slot, i, k):
        return part_copy(d, lax.rem(me_ch + d, n_ch), slot(me_ch, i), k)

    def from_ch(d, slot, i, k):
        peer = lax.rem(me_ch + n_ch - d, n_ch)
        return part_copy(d, peer, slot(peer, i), k)

    def send_part(c):
        for k in range(CHUNK):
            own_part(c * CHUNK + k)
        for d in range(1, n_ch):
            to_ch(d, chunk_slot, c, c).start()

    each(0, chunks // 2, 2, send_part)
    for d in range(1, n_ch):
        cross(d, True).wait_recv()
        for c in range(1, n_col):
            pass_on(d, c, False).start()
    each(chunks // 2, chunks - chunks // 2, 2, send_part)
    for r in range(main, early):
        own_part(r)
    for phase in range(2):
        for q in range(bands):
            for d in range(1, n_ch):
                to_ch(d, piece_slot(phase), q, piece(phase, q)).start()

    for d in range(1, n_ch):
        for c in range(1, n_col):
            pass_on(d, c, True).wait_recv()

    def channel_gram(h):
        block = nc[h].reshape(rank, chans)
        return lax.dot_general(
            block, block, (NT, ((), ())), precision=lax.Precision.HIGHEST,
            preferred_element_type=jnp.float32,
        )

    cg = channel_gram(0)
    for h in range(1, n_ch):
        cg = cg + channel_gram(h)
    cg = stacked(cg)

    def scale_row(r):
        g, s = r // SUB, lax.rem(r, SUB)
        below = product(cg, high[r, pl.ds(0, rank), :], low[r, pl.ds(0, rank), :])
        scale[r] = image_row(ws.at[g], s) / (below + epsilon)

    for r in range(early, rows):
        scale_row(r)
        own_part(r)
    for d in range(1, n_ch):
        peer = lax.rem(me_ch + n_ch - d, n_ch)
        theirs = stacked(nc[peer].reshape(rank, chans))
        for h in range(halves):
            to_early(d, h).wait_recv()
        for r in range(early, rows):
            part[peer, r] = product(theirs, *split(image_row(other.at[d - 1], r - rows + SUB)))

    every = (0, rank)

    def field_side(start, count, band, k):
        def copy(step):
            j, lanes = ((0, cols - LANES), (1, 0))[step < 0]
            return beside(
                step,
                field.at[pl.ds(start + SMOOTH, count), pl.ds(*band), pl.ds(lanes, LANES)],
                sides.at[j, pl.ds(start, count), pl.ds(*band)],
                (c_send.at[j], c_recv.at[j, k]),
            )
        return copy

    def raise_rows(start, count, band, k):
        at = (pl.ds(start, count), pl.ds(*band))
        top = part[(0,) + at]
        for h in range(1, n_ch):
            top = top + part[(h,) + at]
        field[pl.ds(start + SMOOTH, count), pl.ds(*band), pl.ds(0, cols)] = scale[at] * top
        start_pair(field_side(start, count, band, k), me_col, n_col)

    def widen_rows(start, count, band, k):
        receive_pair(field_side(start, count, band, k), me_col, n_col)
        join_rows(start, count, band)

    def join_rows(start, count, band):
        at = (pl.ds(start, count), pl.ds(*band))
        shape = (count * band[1] // SUB, SUB, LANES)
        edge = joined(sides[(0,) + at].reshape(shape), sides[(1,) + at].reshape(shape))
        field[pl.ds(start + SMOOTH, count), pl.ds(*band), pl.ds(cols, LANES)] = edge.reshape(
            count, band[1], LANES
        )

    def raise_chunk(c):
        for k in range(CHUNK):
            scale_row(c * CHUNK + k)
        for d in range(1, n_ch):
            from_ch(d, chunk_slot, c, c).wait_recv()
        raise_rows(c * CHUNK, CHUNK, every, c)

    def widen_chunk(c):
        widen_rows(c * CHUNK, CHUNK, every, c)

    def smooth(source, e, band):
        here, up, down = (
            source[at, pl.ds(*band), :].reshape(band[1] // SUB, SUB, wide)
            for at in (e, e - 1, e + 1)
        )
        total = weight[e, 0] * here + weight[e, 1] * up + weight[e, 2] * down
        total = total + weight[e, 3] * pltpu.roll(here, 1, 2)
        total = total + weight[e, 4] * pltpu.roll(here, wide - 1, 2)
        return total.reshape(band[1], wide)

    def one(e, band=every):
        first[e, pl.ds(*band), :] = smooth(field, e, band)

    def two(e, band=every):
        second[e, pl.ds(*band), :] = smooth(first, e, band)

    def three(e, band=every):
        value = smooth(second, e, band)
        for h in range(halves):
            lines = done.at[h, (e - SMOOTH) // SUB].reshape(rank * SUB, LANES)
            start = band[0] * SUB + lax.rem(e - SMOOTH, SUB)
            lines[pl.ds(start, band[1], stride=SUB), :] = value[:, h * LANES:(h + 1) * LANES]

    def sweep(starts, counts):
        for stage, start, count in zip((one, two, three), starts, counts):
            each(start, count, 2, stage)

    def sweep_chunk(c):
        sweep((CHUNK * c + 2, CHUNK * c + 1, CHUNK * c), (CHUNK,) * 3)

    at_end = chunks + 2 * bands
    edge = early + SMOOTH
    last = rows + SMOOTH
    near = -(-SMOOTH // CHUNK)
    raise_rows(early, EARLY, every, at_end)
    for c in range(near):
        raise_chunk(c)
    widen_rows(early, EARLY, every, at_end)
    for c in range(near):
        widen_chunk(c)
    start_pair(field_across, me_row, n_row)
    for c in range(near, near + 2):
        raise_chunk(c)
    for r in range(main, early):
        scale_row(r)

    def follow(c):
        ends = [CHUNK * (c + 1) + SMOOTH - 1 - i for i in range(3)]
        starts = [max(x - CHUNK, SMOOTH + 1 + i) for i, x in enumerate(ends)]
        sweep(starts, [max(x - y, 0) for x, y in zip(ends, starts)])

    for c in range(near):
        follow(c)

    gathered = gram_row.at[pl.ds(0, n_row - 1)]
    pltpu.make_async_remote_copy(
        gram_in, gram_in, g_send.at[0], g_recv.at[0],
        device_id={"col": lax.rem(me_col + 1, n_col)}, device_id_type=MESH,
    ).wait_send()
    pltpu.make_async_remote_copy(
        gathered, gathered, z_send.at[0], z_recv.at[0],
        device_id={"row": lax.rem(me_row + 1, n_row)}, device_id_type=MESH,
    ).wait_send()
    for c in range(1, n_col):
        spread(c, False, me_ch, c - 1).wait_send()
    for d in range(1, n_ch):
        cross(d, False).wait_send()
        for c in range(1, n_col):
            pass_on(d, c, False).wait_send()
    for d in range(1, n_ch):
        for h in range(halves):
            to_early(d, h).wait_send()
    sent_pair(mark_side, me_col, n_col)
    sent_pair(mark_across, me_row, n_row)

    def step(c, carry):
        widen_chunk(c - 2)
        sweep_chunk(c - 2)
        raise_chunk(c)
        return carry

    clipped = -(-(SMOOTH + 3) // CHUNK) + 2
    for c in range(near + 2, clipped):
        widen_chunk(c - 2)
        follow(c - 2)
        raise_chunk(c)
    middle = (clipped + chunks) // 2 - 1
    lax.fori_loop(clipped, middle, step, 0)
    receive_pair(field_across, me_row, n_row)
    sweep((1, 2, 3), (SMOOTH,) * 3)
    sweep((edge + 1, edge + 2, edge + 3), (last + 1 - edge, last - 1 - edge, max(last - 3 - edge, 0)))
    lax.fori_loop(middle, chunks, step, 0)
    sent_pair(field_across, me_row, n_row)

    def band_of(q):
        return (pl.multiple_of(q * BAND, BAND), BAND)

    def piece_side(phase, q, arriving):
        to_right = odd if phase == 0 else 1 - odd
        peer = me_col + 2 * to_right - 1
        j = to_right if arriving else 1 - to_right
        lanes = pl.ds(pl.multiple_of(to_right * (cols - LANES), LANES), LANES)
        copy = pltpu.make_async_remote_copy(
            field.at[pl.ds(main + SMOOTH, tip), pl.ds(*band_of(q)), lanes],
            sides.at[j, pl.ds(main, tip), pl.ds(*band_of(q))],
            c_send.at[j], c_recv.at[j, piece(phase, q)],
            device_id={"col": lax.rem(peer + n_col, n_col)}, device_id_type=MESH,
        )
        return copy, jnp.logical_and(peer >= 0, peer < n_col)

    def raise_piece(phase, q):
        for d in range(1, n_ch):
            from_ch(d, piece_slot(phase), q, piece(phase, q)).wait_recv()
        at = (pl.ds(main, tip), pl.ds(*band_of(q)), lanes_of(phase))
        top = part[(0,) + at]
        for h in range(1, n_ch):
            top = top + part[(h,) + at]
        field[(pl.ds(main + SMOOTH, tip),) + at[1:]] = scale[at] * top
        copy, there = piece_side(phase, q, False)

        @pl.when(there)
        def _():
            copy.start()

    def finish_band(q):
        band = band_of(q)
        for phase in range(2):
            copy, there = piece_side(phase, q, True)

            @pl.when(there)
            def _():
                copy.wait_recv()

        join_rows(main, tip, band)
        for e in range(main + 2, edge + 1):
            one(e, band)
        for e in range(main + 1, edge + 2):
            two(e, band)
        for e in range(main, min(edge + 3, last)):
            three(e, band)

    widen_chunk(chunks - 2)
    sweep_chunk(chunks - 2)
    def rise(phase):
        def body(q, carry):
            raise_piece(phase, q)
            return carry
        return body

    def finish(q, carry):
        finish_band(q)
        return carry

    lax.fori_loop(0, bands, rise(0), 0)
    widen_chunk(chunks - 1)
    sweep_chunk(chunks - 1)
    lax.fori_loop(0, bands, rise(1), 0)
    lax.fori_loop(0, bands, finish, 0)
    for d in range(1, n_ch):
        whole = part.at[me_ch, pl.ds(0, early)]
        pltpu.make_async_remote_copy(
            whole, whole, t_send.at[d - 1], t_recv.at[d - 1, 0],
            device_id={"ch": lax.rem(me_ch + d, n_ch)}, device_id_type=MESH,
        ).wait_send()

    def all_field_side(step):
        j = int(step < 0)
        return beside(step, sides.at[j], sides.at[j], (c_send.at[j], c_recv.at[j, 0]))

    sent_pair(all_field_side, me_col, n_col)


def store_kernel(done, new_channel, out_hbm, nc_hbm, sem):
    copies = [pltpu.make_async_copy(new_channel, nc_hbm, sem.at[0])]
    halves, groups = done.shape[:2]
    for h in range(halves):
        for g in range(groups):
            target = out_hbm.at[:, pl.ds(g * SUB, SUB), pl.ds(h * LANES, LANES)]
            copies.append(pltpu.make_async_copy(done.at[h, g], target, sem.at[len(copies)]))
    for copy in copies:
        copy.start()
    for copy in copies:
        copy.wait()


def shards(sizes, spectra, pixel_factor, channel_factor, labels):
    n_row, n_col, n_ch = sizes
    rank, rows, cols = pixel_factor.shape
    chans = spectra.shape[0]
    share = rank // n_col
    early = rows - EARLY
    pieces = (early - SMOOTH) // CHUNK + 2 * (rank // BAND)
    tall = rows + 2 * SMOOTH
    wide = cols + LANES
    halves, groups = cols // LANES, rows // SUB
    f32 = jnp.float32
    anywhere = pl.BlockSpec(memory_space=pl.ANY)
    dma = pltpu.SemaphoreType.DMA
    kept = pl.BlockSpec(memory_space=pltpu.VMEM)
    done, new_channel = pl.pallas_call(
        functools.partial(factor_kernel, sizes),
        out_shape=(
            pltpu.VMEM((halves, groups, rank, SUB, LANES), f32),
            pltpu.VMEM(channel_factor.shape, f32),
        ),
        in_specs=[anywhere] * 4,
        out_specs=(kept, kept),
        scratch_shapes=[
            pltpu.VMEM(channel_factor.shape, f32),
            pltpu.VMEM(labels.shape, labels.dtype),
            pltpu.VMEM((groups, halves, chans, SUB, LANES), f32),
            pltpu.VMEM((groups, halves, rank, SUB, LANES), f32),
            pltpu.VMEM((rows, rank + chans, cols), jnp.bfloat16),
            pltpu.VMEM((rows, rank + chans, cols), jnp.bfloat16),
            pltpu.VMEM((n_ch - 1, halves, chans, SUB, LANES), f32),
            pltpu.VMEM((n_col, share, rank + chans), f32),
            pltpu.VMEM((n_col - 1, share, rank + chans), f32),
            pltpu.VMEM((n_row, share, rank + chans), f32),
            pltpu.VMEM((n_ch, n_col, share, chans), f32),
            pltpu.VMEM((n_ch, rows, rank, cols), f32),
            pltpu.VMEM((rows, rank, cols), f32),
            pltpu.VMEM((tall, rank, wide), f32),
            pltpu.VMEM((2, rows, rank, LANES), f32),
            pltpu.VMEM((tall, SUB, wide), f32),
            pltpu.VMEM((rows, SUB, LANES), f32),
            pltpu.VMEM((rows, SUB, LANES), f32),
            pltpu.VMEM((tall, 5, SUB, wide), f32),
            pltpu.VMEM((tall, rank, wide), f32),
            pltpu.VMEM((tall, rank, wide), f32),
            dma((2, halves, groups)),
            dma((n_ch - 1, halves)), dma((n_ch - 1, halves)),
            dma((1,)), dma((n_col - 1,)),
            dma((1,)), dma((n_row - 1,)),
            dma((n_col * n_ch - 1,)), dma((n_col * n_ch - 1,)),
            dma((n_ch - 1,)), dma((n_ch - 1, pieces)),
            dma((2,)), dma((2, pieces + 1)),
            dma((2,)), dma((2,)),
            dma((4,)), dma((4,)),
            dma((2,)),
        ],
        compiler_params=pltpu.CompilerParams(
            collective_id=0, has_side_effects=True, vmem_limit_bytes=52 * 1024 * 1024
        ),
        name="factor",
    )(spectra, pixel_factor, channel_factor, labels)
    return pl.pallas_call(
        store_kernel,
        out_shape=(
            jax.ShapeDtypeStruct(pixel_factor.shape, f32),
            jax.ShapeDtypeStruct(channel_factor.shape, f32),
        ),
        in_specs=[kept, kept],
        out_specs=(anywhere, anywhere),
        scratch_shapes=[dma((halves * groups + 1,))],
        compiler_params=pltpu.CompilerParams(vmem_limit_bytes=4 * 1024 * 1024),
        name="store",
    )(done, new_channel)


def solution(mesh):
    sizes = tuple(mesh.shape[a] for a in ("row", "col", "ch"))
    placed = (P("ch", "row", "col"), P(None, "row", "col"), P(None, "ch"), P("row", "col"))
    return jax.shard_map(
        functools.partial(shards, sizes),
        mesh=mesh,
        in_specs=placed,
        out_specs=(P(None, "row", "col"), P(None, "ch")),
        check_vma=False,
    )
```

```python
import functools

import jax
import jax.numpy as jnp
from jax import lax
from jax.experimental import pallas as pl
from jax.experimental.pallas import tpu as pltpu
from jax.sharding import PartitionSpec as P

SMOOTH = 3
MESH = pl.DeviceIdType.MESH
LANES = 128
SUB = 8
CHUNK = 2
EARLY = 3
BAND = 32

epsilon = 1e-09


def split(value):
    high = value.astype(jnp.bfloat16)
    low = (value - high.astype(jnp.float32)).astype(jnp.bfloat16)
    return high, low


def dot(left, right, contraction):
    return lax.dot_general(
        left, right, (contraction, ((), ())), preferred_element_type=jnp.float32
    )


def dot3(left, right, contraction):
    rows = left[0].shape[0]
    both = dot(jnp.concatenate(left, axis=0), right[0], contraction)
    return both[:rows] + both[rows:] + dot(left[0], right[1], contraction)


NT = ((1,), (1,))
NN = ((1,), (0,))


def each(start, count, width, act):
    def body(i, carry):
        for k in range(width):
            act(start + i * width + k)
        return carry

    whole = count // width
    if whole == 1:
        body(0, 0)
    elif whole:
        lax.fori_loop(0, whole, body, 0)
    for k in range(whole * width, count):
        act(start + k)


def factor_kernel(
    sizes, x_hbm, w_hbm, cf_hbm, lab_hbm, done, nc_out,
    cf_ref, lab_ref, xs, ws, high, low, other, products, gram, gram_in, gram_row, nc, part, scale, field, sides,
    mark, mark_left, mark_right, weight, first, second,
    load_sem, e_send, e_recv, g_send, g_recv, z_send, z_recv, n_send, n_recv,
    t_send, t_recv, c_send, c_recv, r_send, r_recv, m_send, m_recv, small_sem, relay,
):
    n_row, n_col, n_ch = sizes
    rank, rows, cols = w_hbm.shape
    chans = x_hbm.shape[0]
    share = rank // n_col
    early = rows - EARLY
    chunks = (early - SMOOTH) // CHUNK
    main = chunks * CHUNK
    tip = early - main
    bands = rank // BAND
    tall = rows + 2 * SMOOTH
    wide = cols + LANES
    me_row, me_col, me_ch = (lax.axis_index(a) for a in ("row", "col", "ch"))

    halves = cols // LANES
    groups = rows // SUB

    def load(g):
        start = pl.multiple_of(g * SUB, SUB)
        for h in range(halves):
            for j, (source, target) in enumerate(((w_hbm, ws), (x_hbm, xs))):
                yield pltpu.make_async_copy(
                    source.at[:, pl.ds(start, SUB), pl.ds(h * LANES, LANES)],
                    target.at[g, h],
                    load_sem.at[j, h, g],
                )

    def image_row(buffer, s):
        _, depth, _, _ = buffer.shape
        return jnp.concatenate(
            [
                buffer.at[h].reshape(depth * SUB, LANES)[pl.ds(s, depth, stride=SUB), :]
                for h in range(halves)
            ],
            axis=1,
        )

    barrier = pltpu.get_barrier_semaphore()
    def tell(step, semaphore):
        pl.semaphore_signal(
            semaphore, inc=1, device_id={"row": lax.rem(me_row + n_row + step, n_row)},
            device_id_type=MESH,
        )

    def told(step, k):
        return relay.at[int(step < 0), k - 1]

    def known(step, k):
        return me_row >= k if step > 0 else me_row < n_row - k

    def pass_greeting(k):
        for step in (1, -1):
            @pl.when(jnp.logical_and(known(step, k), known(-step, 1)))
            def _():
                tell(step, told(step, k))

    def hear_greeting(k):
        for step in (1, -1):
            @pl.when(known(step, k + 1))
            def _():
                pl.semaphore_wait(told(step, k), 1)

    for step in (1, -1):
        @pl.when(known(-step, 1))
        def _():
            tell(step, barrier)

    for d in range(1, n_col):
        pl.semaphore_signal(
            barrier, inc=1, device_id={"col": lax.rem(me_col + d, n_col)}, device_id_type=MESH
        )
    for d in range(1, n_ch):
        pl.semaphore_signal(
            barrier, inc=1, device_id={"ch": lax.rem(me_ch + d, n_ch)}, device_id_type=MESH
        )

    def to_early(d, h):
        return pltpu.make_async_remote_copy(
            x_hbm.at[:, pl.ds(early, EARLY), pl.ds(h * LANES, LANES)],
            other.at[d - 1, h, :, pl.ds(SUB - EARLY, EARLY), :],
            e_send.at[d - 1, h], e_recv.at[d - 1, h],
            device_id={"ch": lax.rem(me_ch + d, n_ch)}, device_id_type=MESH,
        )

    def beside(step, source, target, at):
        return pltpu.make_async_remote_copy(
            source, target, *at, device_id={"col": lax.rem(me_col + n_col + step, n_col)},
            device_id_type=MESH,
        )

    def mark_side(step):
        k, start, target = ((0, cols - LANES, mark_left), (1, 0, mark_right))[step < 0]
        return beside(
            step, mark.at[pl.ds(SMOOTH, rows), :, pl.ds(start, LANES)], target,
            (m_send.at[k], m_recv.at[k]),
        )

    def across(step, buffer, at):
        start, end = ((rows, 0), (SMOOTH, rows + SMOOTH))[step < 0]
        return pltpu.make_async_remote_copy(
            buffer.at[pl.ds(start, SMOOTH)], buffer.at[pl.ds(end, SMOOTH)], *at,
            device_id={"row": lax.rem(me_row + n_row + step, n_row)}, device_id_type=MESH,
        )

    def mark_across(step):
        k = 2 + (step < 0)
        return across(step, mark, (m_send.at[k], m_recv.at[k]))

    def field_across(step):
        k = int(step < 0)
        return across(step, field, (r_send.at[k], r_recv.at[k]))

    def start_pair(copy, me, n):
        @pl.when(me < n - 1)
        def _():
            copy(1).start()

        @pl.when(me > 0)
        def _():
            copy(-1).start()

    def receive_pair(copy, me, n):
        @pl.when(me > 0)
        def _():
            copy(1).wait_recv()

        @pl.when(me < n - 1)
        def _():
            copy(-1).wait_recv()

    def sent_pair(copy, me, n):
        @pl.when(me < n - 1)
        def _():
            copy(1).wait_send()

        @pl.when(me > 0)
        def _():
            copy(-1).wait_send()

    for copy in load(0):
        copy.start()
    lab_load = pltpu.make_async_copy(lab_hbm, lab_ref, small_sem.at[0])
    cf_load = pltpu.make_async_copy(cf_hbm, cf_ref, small_sem.at[1])
    lab_load.start()
    cf_load.start()
    beside_me = (me_row > 0).astype(jnp.int32) + (me_row < n_row - 1).astype(jnp.int32)
    pl.semaphore_wait(barrier, n_col + n_ch - 2 + beside_me)
    for d in range(1, n_ch):
        for h in range(halves):
            to_early(d, h).start()
    for g in range(1, groups):
        for copy in load(g):
            copy.start()

    for buffer, edge in (
        (sides.at[0], 0), (mark_left, 0), (sides.at[1], n_col - 1), (mark_right, n_col - 1),
    ):

        @pl.when(me_col == edge)
        def _():
            buffer[...] = jnp.zeros(buffer.shape, jnp.float32)

    for at, edge in ((0, 0), (rows + SMOOTH, n_row - 1)):
        for buffer in (field, mark):

            @pl.when(me_row == edge)
            def _():
                buffer[pl.ds(at, SMOOTH)] = jnp.zeros((SMOOTH,) + buffer.shape[1:], jnp.float32)

    lab_load.wait()

    def marks(r):
        row = (lab_ref[pl.ds(r, 1), :] + 1).astype(jnp.float32)
        mark[r + SMOOTH, :, pl.ds(0, cols)] = jnp.broadcast_to(row, (SUB, cols))

    each(0, rows, 8, marks)

    products[...] = jnp.zeros_like(products)

    start_pair(mark_side, me_col, n_col)
    if n_row > 2:
        pass_greeting(1)

    def gather(g, carry):
        for copy in load(g):
            copy.wait()
        sums = [0.0, 0.0]
        for s in range(SUB):
            both = jnp.concatenate([image_row(ws.at[g], s), image_row(xs.at[g], s)], axis=0)
            h, l = split(both)
            high[g * SUB + s] = h
            low[g * SUB + s] = l
            rows_of = jnp.concatenate([h, l[rank:]], axis=0)
            sums[s % 2] = sums[s % 2] + dot(
                rows_of, jnp.concatenate([h[:rank], l[:rank]], axis=0), NT
            )
        products[...] += sums[0] + sums[1]
        return carry

    lax.fori_loop(0, groups, gather, 0)

    w_part = products[pl.ds(0, rank), :]
    first_half = lax.broadcasted_iota(jnp.int32, (1, 2 * rank), 1) < rank
    x_part = products[pl.ds(rank, chans), :] + jnp.where(
        first_half, products[pl.ds(rank + chans, chans), :], 0.0
    )
    turned = jnp.concatenate([w_part, x_part], axis=0).T
    turned = turned[:rank] + turned[rank:]
    gram[...] = turned.reshape(gram.shape)
    swapped = pltpu.roll(w_part, rank, 1)[:, :rank]
    gram[:, :, pl.ds(0, rank)] += swapped.reshape(n_col, share, rank)

    def to_col(d):
        peer = lax.rem(me_col + d, n_col)
        return pltpu.make_async_remote_copy(
            gram.at[peer], gram_in.at[d - 1], g_send.at[0], g_recv.at[d - 1],
            device_id={"col": peer}, device_id_type=MESH,
        )

    for d in range(1, n_col):
        to_col(d).start()
    for k in range(1, n_row - 1):
        hear_greeting(k)
        if k < n_row - 2:
            pass_greeting(k + 1)

    lane = lax.broadcasted_iota(jnp.int32, (1, SUB, LANES), 2)

    def joined(from_left, from_right):
        return jnp.where(
            lane >= LANES - SMOOTH, from_left, jnp.where(lane < SMOOTH, from_right, 0.0)
        )

    receive_pair(mark_side, me_col, n_col)
    mark[pl.ds(SMOOTH, rows), :, pl.ds(cols, LANES)] = joined(mark_left[...], mark_right[...])
    start_pair(mark_across, me_row, n_row)

    own = gram[me_col]
    for d in range(1, n_col):
        to_col(d).wait_recv()
        own = own + gram_in[d - 1]
    gram_row[me_row] = own

    def to_row(d):
        peer = lax.rem(me_row + d, n_row)
        return pltpu.make_async_remote_copy(
            gram_row.at[me_row], gram_row.at[me_row], z_send.at[0], z_recv.at[d - 1],
            device_id={"row": peer}, device_id_type=MESH,
        )

    def from_row(d):
        peer = lax.rem(me_row + n_row - d, n_row)
        return pltpu.make_async_remote_copy(
            gram_row.at[peer], gram_row.at[peer], z_send.at[0], z_recv.at[d - 1],
            device_id={"row": peer}, device_id_type=MESH,
        )

    for d in range(1, n_row):
        to_row(d).start()

    receive_pair(mark_across, me_row, n_row)

    def coefficients(e):
        center = mark[e]
        around = (
            mark[e - 1], mark[e + 1], pltpu.roll(center, 1, 1), pltpu.roll(center, wide - 1, 1)
        )
        parts = [
            jnp.where(near == 0, 0.0, jnp.where(near == center, 1.0, 0.25)) for near in around
        ]
        own_scale = 1.0 / (1.0 + parts[0] + parts[1] + parts[2] + parts[3])
        weight[e, 0] = own_scale
        for j in range(4):
            weight[e, j + 1] = parts[j] * own_scale

    each(1, tall - 2, 4, coefficients)
    cf_load.wait()

    for d in range(1, n_row):
        from_row(d).wait_recv()
    total = gram_row[0]
    for z in range(1, n_row):
        total = total + gram_row[z]
    under = jnp.dot(
        total[:, :rank], cf_ref[...], precision=lax.Precision.HIGHEST,
        preferred_element_type=jnp.float32,
    )
    own_cf = cf_ref[pl.ds(pl.multiple_of(me_col * share, share), share), :]
    nc[me_ch, me_col] = own_cf * total[:, rank:] / (under + epsilon)

    def spread(d, back, h, k):
        col = lax.rem(me_col + (n_col - d if back else 0), n_col)
        slot = nc.at[h, col]
        return pltpu.make_async_remote_copy(
            slot, slot, n_send.at[k], n_recv.at[k],
            device_id={"col": lax.rem(me_col + d, n_col)}, device_id_type=MESH,
        )

    def cross(d, back):
        slot = nc.at[lax.rem(me_ch + (n_ch - d if back else 0), n_ch), me_col]
        k = n_col - 1 + d - 1
        return pltpu.make_async_remote_copy(
            slot, slot, n_send.at[k], n_recv.at[k],
            device_id={"ch": lax.rem(me_ch + d, n_ch)}, device_id_type=MESH,
        )

    def pass_on(d, c, back):
        k = n_col - 1 + n_ch - 1 + (d - 1) * (n_col - 1) + c - 1
        return spread(c, back, lax.rem(me_ch + n_ch - d, n_ch), k)

    for c in range(1, n_col):
        spread(c, False, me_ch, c - 1).start()
    for d in range(1, n_ch):
        cross(d, False).start()
    for c in range(1, n_col):
        spread(c, True, me_ch, c - 1).wait_recv()

    mine = nc[me_ch].reshape(rank, chans)
    nc_out[...] = mine

    def stacked(value):
        h, l = split(value)
        return jnp.concatenate([h, l], axis=0)

    mine = stacked(mine)

    def product(pair, h, l):
        depth = pair.shape[0] // 2
        both = dot(pair, h, NN)
        return both[:depth] + both[depth:] + dot(pair[:depth], l, NN)

    def own_part(r):
        at = (pl.ds(rank, chans), slice(None))
        part[me_ch, r] = product(mine, high[(r,) + at], low[(r,) + at])

    def part_copy(d, peer, slot, k):
        return pltpu.make_async_remote_copy(
            slot, slot, t_send.at[d - 1], t_recv.at[d - 1, k],
            device_id={"ch": peer}, device_id_type=MESH,
        )

    def chunk_slot(h, c):
        return part.at[h, pl.ds(c * CHUNK, CHUNK)]

    odd = lax.rem(me_col, 2)

    def lanes_of(phase):
        if phase == 0:
            return pl.ds(pl.multiple_of(odd * (cols - LANES), LANES), LANES)
        return pl.ds(pl.multiple_of((1 - odd) * LANES, LANES), cols - LANES)

    def piece_slot(phase):
        def slot(h, q):
            band = pl.ds(pl.multiple_of(q * BAND, BAND), BAND)
            return part.at[h, pl.ds(main, tip), band, lanes_of(phase)]
        return slot

    def piece(phase, q):
        return chunks + phase * bands + q

    def to_ch(d, slot, i, k):
        return part_copy(d, lax.rem(me_ch + d, n_ch), slot(me_ch, i), k)

    def from_ch(d, slot, i, k):
        peer = lax.rem(me_ch + n_ch - d, n_ch)
        return part_copy(d, peer, slot(peer, i), k)

    def send_part(c):
        for k in range(CHUNK):
            own_part(c * CHUNK + k)
        for d in range(1, n_ch):
            to_ch(d, chunk_slot, c, c).start()

    each(0, chunks // 2, 2, send_part)
    for d in range(1, n_ch):
        cross(d, True).wait_recv()
        for c in range(1, n_col):
            pass_on(d, c, False).start()
    each(chunks // 2, chunks - chunks // 2, 2, send_part)
    for r in range(main, early):
        own_part(r)
    for phase in range(2):
        for q in range(bands):
            for d in range(1, n_ch):
                to_ch(d, piece_slot(phase), q, piece(phase, q)).start()

    for d in range(1, n_ch):
        for c in range(1, n_col):
            pass_on(d, c, True).wait_recv()

    def channel_gram(h):
        block = nc[h].reshape(rank, chans)
        return lax.dot_general(
            block, block, (NT, ((), ())), precision=lax.Precision.HIGHEST,
            preferred_element_type=jnp.float32,
        )

    cg = channel_gram(0)
    for h in range(1, n_ch):
        cg = cg + channel_gram(h)
    cg = stacked(cg)

    def scale_row(r):
        g, s = r // SUB, lax.rem(r, SUB)
        below = product(cg, high[r, pl.ds(0, rank), :], low[r, pl.ds(0, rank), :])
        scale[r] = image_row(ws.at[g], s) / (below + epsilon)

    for r in range(early, rows):
        scale_row(r)
        own_part(r)
    for d in range(1, n_ch):
        peer = lax.rem(me_ch + n_ch - d, n_ch)
        theirs = stacked(nc[peer].reshape(rank, chans))
        for h in range(halves):
            to_early(d, h).wait_recv()
        for r in range(early, rows):
            part[peer, r] = product(theirs, *split(image_row(other.at[d - 1], r - rows + SUB)))

    every = (0, rank)

    def field_side(start, count, band, k):
        def copy(step):
            j, lanes = ((0, cols - LANES), (1, 0))[step < 0]
            return beside(
                step,
                field.at[pl.ds(start + SMOOTH, count), pl.ds(*band), pl.ds(lanes, LANES)],
                sides.at[j, pl.ds(start, count), pl.ds(*band)],
                (c_send.at[j], c_recv.at[j, k]),
            )
        return copy

    def raise_rows(start, count, band, k):
        at = (pl.ds(start, count), pl.ds(*band))
        top = part[(0,) + at]
        for h in range(1, n_ch):
            top = top + part[(h,) + at]
        field[pl.ds(start + SMOOTH, count), pl.ds(*band), pl.ds(0, cols)] = scale[at] * top
        start_pair(field_side(start, count, band, k), me_col, n_col)

    def widen_rows(start, count, band, k):
        receive_pair(field_side(start, count, band, k), me_col, n_col)
        join_rows(start, count, band)

    def join_rows(start, count, band):
        at = (pl.ds(start, count), pl.ds(*band))
        shape = (count * band[1] // SUB, SUB, LANES)
        edge = joined(sides[(0,) + at].reshape(shape), sides[(1,) + at].reshape(shape))
        field[pl.ds(start + SMOOTH, count), pl.ds(*band), pl.ds(cols, LANES)] = edge.reshape(
            count, band[1], LANES
        )

    def raise_chunk(c):
        for k in range(CHUNK):
            scale_row(c * CHUNK + k)
        for d in range(1, n_ch):
            from_ch(d, chunk_slot, c, c).wait_recv()
        raise_rows(c * CHUNK, CHUNK, every, c)

    def widen_chunk(c):
        widen_rows(c * CHUNK, CHUNK, every, c)

    def smooth(source, e, band):
        here, up, down = (
            source[at, pl.ds(*band), :].reshape(band[1] // SUB, SUB, wide)
            for at in (e, e - 1, e + 1)
        )
        total = weight[e, 0] * here + weight[e, 1] * up + weight[e, 2] * down
        total = total + weight[e, 3] * pltpu.roll(here, 1, 2)
        total = total + weight[e, 4] * pltpu.roll(here, wide - 1, 2)
        return total.reshape(band[1], wide)

    def one(e, band=every):
        first[e, pl.ds(*band), :] = smooth(field, e, band)

    def two(e, band=every):
        second[e, pl.ds(*band), :] = smooth(first, e, band)

    def three(e, band=every):
        value = smooth(second, e, band)
        for h in range(halves):
            lines = done.at[h, (e - SMOOTH) // SUB].reshape(rank * SUB, LANES)
            start = band[0] * SUB + lax.rem(e - SMOOTH, SUB)
            lines[pl.ds(start, band[1], stride=SUB), :] = value[:, h * LANES:(h + 1) * LANES]

    def sweep(starts, counts):
        for stage, start, count in zip((one, two, three), starts, counts):
            each(start, count, 2, stage)

    def sweep_chunk(c):
        sweep((CHUNK * c + 2, CHUNK * c + 1, CHUNK * c), (CHUNK,) * 3)

    at_end = chunks + 2 * bands
    edge = early + SMOOTH
    last = rows + SMOOTH
    near = -(-SMOOTH // CHUNK)
    raise_rows(early, EARLY, every, at_end)
    for c in range(near):
        raise_chunk(c)
    widen_rows(early, EARLY, every, at_end)
    for c in range(near):
        widen_chunk(c)
    start_pair(field_across, me_row, n_row)
    for c in range(near, near + 2):
        raise_chunk(c)
    for r in range(main, early):
        scale_row(r)

    def follow(c):
        ends = [CHUNK * (c + 1) + SMOOTH - 1 - i for i in range(3)]
        starts = [max(x - CHUNK, SMOOTH + 1 + i) for i, x in enumerate(ends)]
        sweep(starts, [max(x - y, 0) for x, y in zip(ends, starts)])

    for c in range(near):
        follow(c)

    gathered = gram_row.at[pl.ds(0, n_row - 1)]
    pltpu.make_async_remote_copy(
        gram_in, gram_in, g_send.at[0], g_recv.at[0],
        device_id={"col": lax.rem(me_col + 1, n_col)}, device_id_type=MESH,
    ).wait_send()
    pltpu.make_async_remote_copy(
        gathered, gathered, z_send.at[0], z_recv.at[0],
        device_id={"row": lax.rem(me_row + 1, n_row)}, device_id_type=MESH,
    ).wait_send()
    for c in range(1, n_col):
        spread(c, False, me_ch, c - 1).wait_send()
    for d in range(1, n_ch):
        cross(d, False).wait_send()
        for c in range(1, n_col):
            pass_on(d, c, False).wait_send()
    for d in range(1, n_ch):
        for h in range(halves):
            to_early(d, h).wait_send()
    sent_pair(mark_side, me_col, n_col)
    sent_pair(mark_across, me_row, n_row)

    def step(c, carry):
        widen_chunk(c - 2)
        sweep_chunk(c - 2)
        raise_chunk(c)
        return carry

    clipped = -(-(SMOOTH + 3) // CHUNK) + 2
    for c in range(near + 2, clipped):
        widen_chunk(c - 2)
        follow(c - 2)
        raise_chunk(c)
    middle = (clipped + chunks) // 2 - 1
    lax.fori_loop(clipped, middle, step, 0)
    receive_pair(field_across, me_row, n_row)
    sweep((1, 2, 3), (SMOOTH,) * 3)
    sweep((edge + 1, edge + 2, edge + 3), (last + 1 - edge, last - 1 - edge, max(last - 3 - edge, 0)))
    lax.fori_loop(middle, chunks, step, 0)
    sent_pair(field_across, me_row, n_row)

    def band_of(q):
        return (pl.multiple_of(q * BAND, BAND), BAND)

    def piece_side(phase, q, arriving):
        to_right = odd if phase == 0 else 1 - odd
        peer = me_col + 2 * to_right - 1
        j = to_right if arriving else 1 - to_right
        lanes = pl.ds(pl.multiple_of(to_right * (cols - LANES), LANES), LANES)
        copy = pltpu.make_async_remote_copy(
            field.at[pl.ds(main + SMOOTH, tip), pl.ds(*band_of(q)), lanes],
            sides.at[j, pl.ds(main, tip), pl.ds(*band_of(q))],
            c_send.at[j], c_recv.at[j, piece(phase, q)],
            device_id={"col": lax.rem(peer + n_col, n_col)}, device_id_type=MESH,
        )
        return copy, jnp.logical_and(peer >= 0, peer < n_col)

    def raise_piece(phase, q):
        for d in range(1, n_ch):
            from_ch(d, piece_slot(phase), q, piece(phase, q)).wait_recv()
        at = (pl.ds(main, tip), pl.ds(*band_of(q)), lanes_of(phase))
        top = part[(0,) + at]
        for h in range(1, n_ch):
            top = top + part[(h,) + at]
        field[(pl.ds(main + SMOOTH, tip),) + at[1:]] = scale[at] * top
        copy, there = piece_side(phase, q, False)

        @pl.when(there)
        def _():
            copy.start()

    def finish_band(q):
        band = band_of(q)
        for phase in range(2):
            copy, there = piece_side(phase, q, True)

            @pl.when(there)
            def _():
                copy.wait_recv()

        join_rows(main, tip, band)
        for e in range(main + 2, edge + 1):
            one(e, band)
        for e in range(main + 1, edge + 2):
            two(e, band)
        for e in range(main, min(edge + 3, last)):
            three(e, band)

    widen_chunk(chunks - 2)
    sweep_chunk(chunks - 2)
    def rise(phase):
        def body(q, carry):
            raise_piece(phase, q)
            return carry
        return body

    def finish(q, carry):
        finish_band(q)
        return carry

    lax.fori_loop(0, bands, rise(0), 0)
    widen_chunk(chunks - 1)
    sweep_chunk(chunks - 1)
    lax.fori_loop(0, bands, rise(1), 0)
    lax.fori_loop(0, bands, finish, 0)
    for d in range(1, n_ch):
        whole = part.at[me_ch, pl.ds(0, early)]
        pltpu.make_async_remote_copy(
            whole, whole, t_send.at[d - 1], t_recv.at[d - 1, 0],
            device_id={"ch": lax.rem(me_ch + d, n_ch)}, device_id_type=MESH,
        ).wait_send()

    def all_field_side(step):
        j = int(step < 0)
        return beside(step, sides.at[j], sides.at[j], (c_send.at[j], c_recv.at[j, 0]))

    sent_pair(all_field_side, me_col, n_col)


def store_kernel(done, new_channel, out_hbm, nc_hbm, sem):
    copies = [pltpu.make_async_copy(new_channel, nc_hbm, sem.at[0])]
    halves, groups = done.shape[:2]
    for h in range(halves):
        for g in range(groups):
            target = out_hbm.at[:, pl.ds(g * SUB, SUB), pl.ds(h * LANES, LANES)]
            copies.append(pltpu.make_async_copy(done.at[h, g], target, sem.at[len(copies)]))
    for copy in copies:
        copy.start()
    for copy in copies:
        copy.wait()


def shards(sizes, spectra, pixel_factor, channel_factor, labels):
    n_row, n_col, n_ch = sizes
    rank, rows, cols = pixel_factor.shape
    chans = spectra.shape[0]
    share = rank // n_col
    early = rows - EARLY
    pieces = (early - SMOOTH) // CHUNK + 2 * (rank // BAND)
    tall = rows + 2 * SMOOTH
    wide = cols + LANES
    halves, groups = cols // LANES, rows // SUB
    f32 = jnp.float32
    anywhere = pl.BlockSpec(memory_space=pl.ANY)
    dma = pltpu.SemaphoreType.DMA
    kept = pl.BlockSpec(memory_space=pltpu.VMEM)
    done, new_channel = pl.pallas_call(
        functools.partial(factor_kernel, sizes),
        out_shape=(
            pltpu.VMEM((halves, groups, rank, SUB, LANES), f32),
            pltpu.VMEM(channel_factor.shape, f32),
        ),
        in_specs=[anywhere] * 4,
        out_specs=(kept, kept),
        scratch_shapes=[
            pltpu.VMEM(channel_factor.shape, f32),
            pltpu.VMEM(labels.shape, labels.dtype),
            pltpu.VMEM((groups, halves, chans, SUB, LANES), f32),
            pltpu.VMEM((groups, halves, rank, SUB, LANES), f32),
            pltpu.VMEM((rows, rank + chans, cols), jnp.bfloat16),
            pltpu.VMEM((rows, rank + chans, cols), jnp.bfloat16),
            pltpu.VMEM((n_ch - 1, halves, chans, SUB, LANES), f32),
            pltpu.VMEM((rank + 2 * chans, 2 * rank), f32),
            pltpu.VMEM((n_col, share, rank + chans), f32),
            pltpu.VMEM((n_col - 1, share, rank + chans), f32),
            pltpu.VMEM((n_row, share, rank + chans), f32),
            pltpu.VMEM((n_ch, n_col, share, chans), f32),
            pltpu.VMEM((n_ch, rows, rank, cols), f32),
            pltpu.VMEM((rows, rank, cols), f32),
            pltpu.VMEM((tall, rank, wide), f32),
            pltpu.VMEM((2, rows, rank, LANES), f32),
            pltpu.VMEM((tall, SUB, wide), f32),
            pltpu.VMEM((rows, SUB, LANES), f32),
            pltpu.VMEM((rows, SUB, LANES), f32),
            pltpu.VMEM((tall, 5, SUB, wide), f32),
            pltpu.VMEM((tall, rank, wide), f32),
            pltpu.VMEM((tall, rank, wide), f32),
            dma((2, halves, groups)),
            dma((n_ch - 1, halves)), dma((n_ch - 1, halves)),
            dma((1,)), dma((n_col - 1,)),
            dma((1,)), dma((n_row - 1,)),
            dma((n_col * n_ch - 1,)), dma((n_col * n_ch - 1,)),
            dma((n_ch - 1,)), dma((n_ch - 1, pieces)),
            dma((2,)), dma((2, pieces + 1)),
            dma((2,)), dma((2,)),
            dma((4,)), dma((4,)),
            dma((2,)),
            pltpu.SemaphoreType.REGULAR((2, max(n_row - 2, 1))),
        ],
        compiler_params=pltpu.CompilerParams(
            collective_id=0, has_side_effects=True, vmem_limit_bytes=52 * 1024 * 1024
        ),
        name="factor",
    )(spectra, pixel_factor, channel_factor, labels)
    return pl.pallas_call(
        store_kernel,
        out_shape=(
            jax.ShapeDtypeStruct(pixel_factor.shape, f32),
            jax.ShapeDtypeStruct(channel_factor.shape, f32),
        ),
        in_specs=[kept, kept],
        out_specs=(anywhere, anywhere),
        scratch_shapes=[dma((halves * groups + 1,))],
        compiler_params=pltpu.CompilerParams(vmem_limit_bytes=4 * 1024 * 1024),
        name="store",
    )(done, new_channel)


def solution(mesh):
    sizes = tuple(mesh.shape[a] for a in ("row", "col", "ch"))
    placed = (P("ch", "row", "col"), P(None, "row", "col"), P(None, "ch"), P("row", "col"))
    return jax.shard_map(
        functools.partial(shards, sizes),
        mesh=mesh,
        in_specs=placed,
        out_specs=(P(None, "row", "col"), P(None, "ch")),
        check_vma=False,
    )
```

```python
import functools

import jax
import jax.numpy as jnp
from jax import lax
from jax.experimental import pallas as pl
from jax.experimental.pallas import tpu as pltpu
from jax.sharding import PartitionSpec as P

SMOOTH = 3
MESH = pl.DeviceIdType.MESH
LANES = 128
SUB = 8
CHUNK = 2
EARLY = 3
HALVES = 2
BAND = 16

epsilon = 1e-09


def split(value):
    high = value.astype(jnp.bfloat16)
    low = (value - high.astype(jnp.float32)).astype(jnp.bfloat16)
    return high, low


def dot(left, right, contraction):
    return lax.dot_general(
        left, right, (contraction, ((), ())), preferred_element_type=jnp.float32
    )


def dot3(left, right, contraction):
    rows = left[0].shape[0]
    both = dot(jnp.concatenate(left, axis=0), right[0], contraction)
    return both[:rows] + both[rows:] + dot(left[0], right[1], contraction)


NT = ((1,), (1,))
NN = ((1,), (0,))


def each(start, count, width, act):
    def body(i, carry):
        for k in range(width):
            act(start + i * width + k)
        return carry

    whole = count // width
    if whole == 1:
        body(0, 0)
    elif whole:
        lax.fori_loop(0, whole, body, 0)
    for k in range(whole * width, count):
        act(start + k)


def factor_kernel(
    sizes, x_hbm, w_hbm, cf_hbm, lab_hbm, done, nc_out,
    cf_ref, lab_ref, xs, ws, high, low, other, products, gram, gram_in, gram_row, nc, part, scale, field, sides,
    mark, mark_left, mark_right, weight, first, second,
    load_sem, e_send, e_recv, g_send, g_recv, z_send, z_recv, n_send, n_recv,
    t_send, t_recv, c_send, c_recv, r_send, r_recv, m_send, m_recv, small_sem, relay,
):
    n_row, n_col, n_ch = sizes
    rank, rows, cols = w_hbm.shape
    chans = x_hbm.shape[0]
    share = rank // n_col
    early = rows - EARLY
    chunks = (early - SMOOTH) // CHUNK
    main = chunks * CHUNK
    tip = early - main
    bands = rank // BAND
    tall = rows + 2 * SMOOTH
    wide = cols + LANES
    me_row, me_col, me_ch = (lax.axis_index(a) for a in ("row", "col", "ch"))

    halves = cols // LANES
    groups = rows // SUB

    def load(g):
        start = pl.multiple_of(g * SUB, SUB)
        for h in range(halves):
            for j, (source, target) in enumerate(((w_hbm, ws), (x_hbm, xs))):
                yield pltpu.make_async_copy(
                    source.at[:, pl.ds(start, SUB), pl.ds(h * LANES, LANES)],
                    target.at[g, h],
                    load_sem.at[j, h, g],
                )

    def image_row(buffer, s):
        _, depth, _, _ = buffer.shape
        return jnp.concatenate(
            [
                buffer.at[h].reshape(depth * SUB, LANES)[pl.ds(s, depth, stride=SUB), :]
                for h in range(halves)
            ],
            axis=1,
        )

    barrier = pltpu.get_barrier_semaphore()
    def tell(step, semaphore):
        pl.semaphore_signal(
            semaphore, inc=1, device_id={"row": lax.rem(me_row + n_row + step, n_row)},
            device_id_type=MESH,
        )

    def told(step, k):
        return relay.at[int(step < 0), k - 1]

    def known(step, k):
        return me_row >= k if step > 0 else me_row < n_row - k

    def pass_greeting(k):
        for step in (1, -1):
            @pl.when(jnp.logical_and(known(step, k), known(-step, 1)))
            def _():
                tell(step, told(step, k))

    def hear_greeting(k):
        for step in (1, -1):
            @pl.when(known(step, k + 1))
            def _():
                pl.semaphore_wait(told(step, k), 1)

    for step in (1, -1):
        @pl.when(known(-step, 1))
        def _():
            tell(step, barrier)

    for d in range(1, n_col):
        pl.semaphore_signal(
            barrier, inc=1, device_id={"col": lax.rem(me_col + d, n_col)}, device_id_type=MESH
        )
    for d in range(1, n_ch):
        pl.semaphore_signal(
            barrier, inc=1, device_id={"ch": lax.rem(me_ch + d, n_ch)}, device_id_type=MESH
        )

    def to_early(d, h):
        return pltpu.make_async_remote_copy(
            x_hbm.at[:, pl.ds(early, EARLY), pl.ds(h * LANES, LANES)],
            other.at[d - 1, h, :, pl.ds(SUB - EARLY, EARLY), :],
            e_send.at[d - 1, h], e_recv.at[d - 1, h],
            device_id={"ch": lax.rem(me_ch + d, n_ch)}, device_id_type=MESH,
        )

    def beside(step, source, target, at):
        return pltpu.make_async_remote_copy(
            source, target, *at, device_id={"col": lax.rem(me_col + n_col + step, n_col)},
            device_id_type=MESH,
        )

    def mark_side(step):
        k, start, target = ((0, cols - LANES, mark_left), (1, 0, mark_right))[step < 0]
        return beside(
            step, mark.at[pl.ds(SMOOTH, rows), :, pl.ds(start, LANES)], target,
            (m_send.at[k], m_recv.at[k]),
        )

    def across(step, buffer, at):
        start, end = ((rows, 0), (SMOOTH, rows + SMOOTH))[step < 0]
        return pltpu.make_async_remote_copy(
            buffer.at[pl.ds(start, SMOOTH)], buffer.at[pl.ds(end, SMOOTH)], *at,
            device_id={"row": lax.rem(me_row + n_row + step, n_row)}, device_id_type=MESH,
        )

    def mark_across(step):
        k = 2 + (step < 0)
        return across(step, mark, (m_send.at[k], m_recv.at[k]))

    def field_across(step):
        k = int(step < 0)
        return across(step, field, (r_send.at[k], r_recv.at[k]))

    def start_pair(copy, me, n):
        @pl.when(me < n - 1)
        def _():
            copy(1).start()

        @pl.when(me > 0)
        def _():
            copy(-1).start()

    def receive_pair(copy, me, n):
        @pl.when(me > 0)
        def _():
            copy(1).wait_recv()

        @pl.when(me < n - 1)
        def _():
            copy(-1).wait_recv()

    def sent_pair(copy, me, n):
        @pl.when(me < n - 1)
        def _():
            copy(1).wait_send()

        @pl.when(me > 0)
        def _():
            copy(-1).wait_send()

    for copy in load(0):
        copy.start()
    lab_load = pltpu.make_async_copy(lab_hbm, lab_ref, small_sem.at[0])
    cf_load = pltpu.make_async_copy(cf_hbm, cf_ref, small_sem.at[1])
    lab_load.start()
    cf_load.start()
    beside_me = (me_row > 0).astype(jnp.int32) + (me_row < n_row - 1).astype(jnp.int32)
    pl.semaphore_wait(barrier, n_col + n_ch - 2 + beside_me)
    for d in range(1, n_ch):
        for h in range(halves):
            to_early(d, h).start()
    for g in range(1, groups):
        for copy in load(g):
            copy.start()

    for buffer, edge in (
        (sides.at[0], 0), (mark_left, 0), (sides.at[1], n_col - 1), (mark_right, n_col - 1),
    ):

        @pl.when(me_col == edge)
        def _():
            buffer[...] = jnp.zeros(buffer.shape, jnp.float32)

    for at, edge in ((0, 0), (rows + SMOOTH, n_row - 1)):
        for buffer in (field, mark):

            @pl.when(me_row == edge)
            def _():
                buffer[pl.ds(at, SMOOTH)] = jnp.zeros((SMOOTH,) + buffer.shape[1:], jnp.float32)

    lab_load.wait()

    def marks(r):
        row = (lab_ref[pl.ds(r, 1), :] + 1).astype(jnp.float32)
        mark[r + SMOOTH, :, pl.ds(0, cols)] = jnp.broadcast_to(row, (SUB, cols))

    each(0, rows, 8, marks)

    products[...] = jnp.zeros_like(products)

    start_pair(mark_side, me_col, n_col)
    if n_row > 2:
        pass_greeting(1)

    def gather(g, carry):
        for copy in load(g):
            copy.wait()
        sums = [0.0, 0.0]
        for s in range(SUB):
            both = jnp.concatenate([image_row(ws.at[g], s), image_row(xs.at[g], s)], axis=0)
            h, l = split(both)
            high[g * SUB + s] = h
            low[g * SUB + s] = l
            rows_of = jnp.concatenate([h, l[rank:]], axis=0)
            sums[s % 2] = sums[s % 2] + dot(
                rows_of, jnp.concatenate([h[:rank], l[:rank]], axis=0), NT
            )
        products[...] += sums[0] + sums[1]
        return carry

    lax.fori_loop(0, groups, gather, 0)

    w_part = products[pl.ds(0, rank), :]
    first_half = lax.broadcasted_iota(jnp.int32, (1, 2 * rank), 1) < rank
    x_part = products[pl.ds(rank, chans), :] + jnp.where(
        first_half, products[pl.ds(rank + chans, chans), :], 0.0
    )
    turned = jnp.concatenate([w_part, x_part], axis=0).T
    turned = turned[:rank] + turned[rank:]
    gram[...] = turned.reshape(gram.shape)
    swapped = pltpu.roll(w_part, rank, 1)[:, :rank]
    gram[:, :, pl.ds(0, rank)] += swapped.reshape(n_col, share, rank)

    lines = share // HALVES

    def half(k):
        return pl.ds(k * lines, lines)

    def to_col(d, k):
        peer = lax.rem(me_col + d, n_col)
        return pltpu.make_async_remote_copy(
            gram.at[peer, half(k)], gram_in.at[d - 1, half(k)], g_send.at[0], g_recv.at[d - 1, k],
            device_id={"col": peer}, device_id_type=MESH,
        )

    for k in range(HALVES):
        for d in range(1, n_col):
            to_col(d, k).start()
    for k in range(1, n_row - 1):
        hear_greeting(k)
        if k < n_row - 2:
            pass_greeting(k + 1)

    lane = lax.broadcasted_iota(jnp.int32, (1, SUB, LANES), 2)

    def joined(from_left, from_right):
        return jnp.where(
            lane >= LANES - SMOOTH, from_left, jnp.where(lane < SMOOTH, from_right, 0.0)
        )

    receive_pair(mark_side, me_col, n_col)
    mark[pl.ds(SMOOTH, rows), :, pl.ds(cols, LANES)] = joined(mark_left[...], mark_right[...])
    start_pair(mark_across, me_row, n_row)

    def along_row(d, back, k):
        at = lax.rem(me_row + (n_row - d if back else 0), n_row)
        slot = gram_row.at[at, half(k)]
        return pltpu.make_async_remote_copy(
            slot, slot, z_send.at[0], z_recv.at[d - 1, k],
            device_id={"row": lax.rem(me_row + d, n_row)}, device_id_type=MESH,
        )

    for k in range(HALVES):
        own = gram[me_col, half(k)]
        for d in range(1, n_col):
            to_col(d, k).wait_recv()
            own = own + gram_in[d - 1, half(k)]
        gram_row[me_row, half(k)] = own
        for d in range(1, n_row):
            along_row(d, False, k).start()

    receive_pair(mark_across, me_row, n_row)

    def coefficients(e):
        center = mark[e]
        around = (
            mark[e - 1], mark[e + 1], pltpu.roll(center, 1, 1), pltpu.roll(center, wide - 1, 1)
        )
        parts = [
            jnp.where(near == 0, 0.0, jnp.where(near == center, 1.0, 0.25)) for near in around
        ]
        own_scale = 1.0 / (1.0 + parts[0] + parts[1] + parts[2] + parts[3])
        weight[e, 0] = own_scale
        for j in range(4):
            weight[e, j + 1] = parts[j] * own_scale

    each(1, tall - 2, 4, coefficients)
    cf_load.wait()

    def spread(d, back, h, k, part_of=slice(None)):
        col = lax.rem(me_col + (n_col - d if back else 0), n_col)
        slot = nc.at[h, col, part_of]
        return pltpu.make_async_remote_copy(
            slot, slot, n_send.at[k], n_recv.at[k],
            device_id={"col": lax.rem(me_col + d, n_col)}, device_id_type=MESH,
        )

    def spread_half(c, back, k):
        return spread(c, back, me_ch, (c - 1) * HALVES + k, half(k))

    first_cross = (n_col - 1) * HALVES

    def cross(d, back):
        slot = nc.at[lax.rem(me_ch + (n_ch - d if back else 0), n_ch), me_col]
        k = first_cross + d - 1
        return pltpu.make_async_remote_copy(
            slot, slot, n_send.at[k], n_recv.at[k],
            device_id={"ch": lax.rem(me_ch + d, n_ch)}, device_id_type=MESH,
        )

    def pass_on(d, c, back):
        k = first_cross + n_ch - 1 + (d - 1) * (n_col - 1) + c - 1
        return spread(c, back, lax.rem(me_ch + n_ch - d, n_ch), k)

    for k in range(HALVES):
        for d in range(1, n_row):
            along_row(d, True, k).wait_recv()
        total = gram_row[0, half(k)]
        for z in range(1, n_row):
            total = total + gram_row[z, half(k)]
        under = jnp.dot(
            total[:, :rank], cf_ref[...], precision=lax.Precision.HIGHEST,
            preferred_element_type=jnp.float32,
        )
        start = pl.multiple_of(me_col * share + k * lines, lines)
        own_cf = cf_ref[pl.ds(start, lines), :]
        nc[me_ch, me_col, half(k)] = own_cf * total[:, rank:] / (under + epsilon)
        for c in range(1, n_col):
            spread_half(c, False, k).start()
    for d in range(1, n_ch):
        cross(d, False).start()
    for k in range(HALVES):
        for c in range(1, n_col):
            spread_half(c, True, k).wait_recv()

    mine = nc[me_ch].reshape(rank, chans)
    nc_out[...] = mine

    def stacked(value):
        h, l = split(value)
        return jnp.concatenate([h, l], axis=0)

    mine = stacked(mine)

    def product(pair, h, l):
        depth = pair.shape[0] // 2
        both = dot(pair, h, NN)
        return both[:depth] + both[depth:] + dot(pair[:depth], l, NN)

    def own_part(r):
        at = (pl.ds(rank, chans), slice(None))
        part[me_ch, r] = product(mine, high[(r,) + at], low[(r,) + at])

    def part_copy(d, peer, slot, k):
        return pltpu.make_async_remote_copy(
            slot, slot, t_send.at[d - 1], t_recv.at[d - 1, k],
            device_id={"ch": peer}, device_id_type=MESH,
        )

    def chunk_slot(h, c):
        return part.at[h, pl.ds(c * CHUNK, CHUNK)]

    odd = lax.rem(me_col, 2)

    def lanes_of(phase):
        if phase == 0:
            return pl.ds(pl.multiple_of(odd * (cols - LANES), LANES), LANES)
        return pl.ds(pl.multiple_of((1 - odd) * LANES, LANES), cols - LANES)

    def piece_slot(phase):
        def slot(h, q):
            band = pl.ds(pl.multiple_of(q * BAND, BAND), BAND)
            return part.at[h, pl.ds(main, tip), band, lanes_of(phase)]
        return slot

    def piece(phase, q):
        return chunks + phase * bands + q

    def to_ch(d, slot, i, k):
        return part_copy(d, lax.rem(me_ch + d, n_ch), slot(me_ch, i), k)

    def from_ch(d, slot, i, k):
        peer = lax.rem(me_ch + n_ch - d, n_ch)
        return part_copy(d, peer, slot(peer, i), k)

    def send_part(c):
        for k in range(CHUNK):
            own_part(c * CHUNK + k)
        for d in range(1, n_ch):
            to_ch(d, chunk_slot, c, c).start()

    each(0, chunks // 2, 2, send_part)
    for d in range(1, n_ch):
        cross(d, True).wait_recv()
        for c in range(1, n_col):
            pass_on(d, c, False).start()
    each(chunks // 2, chunks - chunks // 2, 2, send_part)
    for r in range(main, early):
        own_part(r)
    for phase in range(2):
        for q in range(bands):
            for d in range(1, n_ch):
                to_ch(d, piece_slot(phase), q, piece(phase, q)).start()

    for d in range(1, n_ch):
        for c in range(1, n_col):
            pass_on(d, c, True).wait_recv()

    def channel_gram(h):
        block = nc[h].reshape(rank, chans)
        return lax.dot_general(
            block, block, (NT, ((), ())), precision=lax.Precision.HIGHEST,
            preferred_element_type=jnp.float32,
        )

    cg = channel_gram(0)
    for h in range(1, n_ch):
        cg = cg + channel_gram(h)
    cg = stacked(cg)

    def scale_row(r):
        g, s = r // SUB, lax.rem(r, SUB)
        below = product(cg, high[r, pl.ds(0, rank), :], low[r, pl.ds(0, rank), :])
        scale[r] = image_row(ws.at[g], s) / (below + epsilon)

    for r in range(early, rows):
        scale_row(r)
        own_part(r)
    for d in range(1, n_ch):
        peer = lax.rem(me_ch + n_ch - d, n_ch)
        theirs = stacked(nc[peer].reshape(rank, chans))
        for h in range(halves):
            to_early(d, h).wait_recv()
        for r in range(early, rows):
            part[peer, r] = product(theirs, *split(image_row(other.at[d - 1], r - rows + SUB)))

    every = (0, rank)

    def field_side(start, count, band, k):
        def copy(step):
            j, lanes = ((0, cols - LANES), (1, 0))[step < 0]
            return beside(
                step,
                field.at[pl.ds(start + SMOOTH, count), pl.ds(*band), pl.ds(lanes, LANES)],
                sides.at[j, pl.ds(start, count), pl.ds(*band)],
                (c_send.at[j], c_recv.at[j, k]),
            )
        return copy

    def raise_rows(start, count, band, k):
        at = (pl.ds(start, count), pl.ds(*band))
        top = part[(0,) + at]
        for h in range(1, n_ch):
            top = top + part[(h,) + at]
        field[pl.ds(start + SMOOTH, count), pl.ds(*band), pl.ds(0, cols)] = scale[at] * top
        start_pair(field_side(start, count, band, k), me_col, n_col)

    def widen_rows(start, count, band, k):
        receive_pair(field_side(start, count, band, k), me_col, n_col)
        join_rows(start, count, band)

    def join_rows(start, count, band):
        at = (pl.ds(start, count), pl.ds(*band))
        shape = (count * band[1] // SUB, SUB, LANES)
        edge = joined(sides[(0,) + at].reshape(shape), sides[(1,) + at].reshape(shape))
        field[pl.ds(start + SMOOTH, count), pl.ds(*band), pl.ds(cols, LANES)] = edge.reshape(
            count, band[1], LANES
        )

    def raise_chunk(c):
        for k in range(CHUNK):
            scale_row(c * CHUNK + k)
        for d in range(1, n_ch):
            from_ch(d, chunk_slot, c, c).wait_recv()
        raise_rows(c * CHUNK, CHUNK, every, c)

    def widen_chunk(c):
        widen_rows(c * CHUNK, CHUNK, every, c)

    def smooth(source, e, band):
        here, up, down = (
            source[at, pl.ds(*band), :].reshape(band[1] // SUB, SUB, wide)
            for at in (e, e - 1, e + 1)
        )
        total = weight[e, 0] * here + weight[e, 1] * up + weight[e, 2] * down
        total = total + weight[e, 3] * pltpu.roll(here, 1, 2)
        total = total + weight[e, 4] * pltpu.roll(here, wide - 1, 2)
        return total.reshape(band[1], wide)

    def one(e, band=every):
        first[e, pl.ds(*band), :] = smooth(field, e, band)

    def two(e, band=every):
        second[e, pl.ds(*band), :] = smooth(first, e, band)

    def three(e, band=every):
        value = smooth(second, e, band)
        for h in range(halves):
            lines = done.at[h, (e - SMOOTH) // SUB].reshape(rank * SUB, LANES)
            start = band[0] * SUB + lax.rem(e - SMOOTH, SUB)
            lines[pl.ds(start, band[1], stride=SUB), :] = value[:, h * LANES:(h + 1) * LANES]

    def sweep(starts, counts):
        for stage, start, count in zip((one, two, three), starts, counts):
            each(start, count, 2, stage)

    def sweep_chunk(c):
        sweep((CHUNK * c + 2, CHUNK * c + 1, CHUNK * c), (CHUNK,) * 3)

    at_end = chunks + 2 * bands
    edge = early + SMOOTH
    last = rows + SMOOTH
    near = -(-SMOOTH // CHUNK)
    raise_rows(early, EARLY, every, at_end)
    for c in range(near):
        raise_chunk(c)
    widen_rows(early, EARLY, every, at_end)
    for c in range(near):
        widen_chunk(c)
    start_pair(field_across, me_row, n_row)
    for c in range(near, near + 2):
        raise_chunk(c)
    for r in range(main, early):
        scale_row(r)

    def follow(c):
        ends = [CHUNK * (c + 1) + SMOOTH - 1 - i for i in range(3)]
        starts = [max(x - CHUNK, SMOOTH + 1 + i) for i, x in enumerate(ends)]
        sweep(starts, [max(x - y, 0) for x, y in zip(ends, starts)])

    for c in range(near):
        follow(c)

    gathered = gram_row.at[pl.ds(0, n_row - 1)]
    pltpu.make_async_remote_copy(
        gram_in, gram_in, g_send.at[0], g_recv.at[0, 0],
        device_id={"col": lax.rem(me_col + 1, n_col)}, device_id_type=MESH,
    ).wait_send()
    pltpu.make_async_remote_copy(
        gathered, gathered, z_send.at[0], z_recv.at[0, 0],
        device_id={"row": lax.rem(me_row + 1, n_row)}, device_id_type=MESH,
    ).wait_send()
    for k in range(HALVES):
        for c in range(1, n_col):
            spread_half(c, False, k).wait_send()
    for d in range(1, n_ch):
        cross(d, False).wait_send()
        for c in range(1, n_col):
            pass_on(d, c, False).wait_send()
    for d in range(1, n_ch):
        for h in range(halves):
            to_early(d, h).wait_send()
    sent_pair(mark_side, me_col, n_col)
    sent_pair(mark_across, me_row, n_row)

    def step(c, carry):
        widen_chunk(c - 2)
        sweep_chunk(c - 2)
        raise_chunk(c)
        return carry

    clipped = -(-(SMOOTH + 3) // CHUNK) + 2
    for c in range(near + 2, clipped):
        widen_chunk(c - 2)
        follow(c - 2)
        raise_chunk(c)
    middle = (clipped + chunks) // 2 - 1
    lax.fori_loop(clipped, middle, step, 0)
    receive_pair(field_across, me_row, n_row)
    sweep((1, 2, 3), (SMOOTH,) * 3)
    sweep((edge + 1, edge + 2, edge + 3), (last + 1 - edge, last - 1 - edge, max(last - 3 - edge, 0)))
    lax.fori_loop(middle, chunks, step, 0)
    sent_pair(field_across, me_row, n_row)

    def band_of(q):
        return (pl.multiple_of(q * BAND, BAND), BAND)

    def piece_side(phase, q, arriving):
        to_right = odd if phase == 0 else 1 - odd
        peer = me_col + 2 * to_right - 1
        j = to_right if arriving else 1 - to_right
        lanes = pl.ds(pl.multiple_of(to_right * (cols - LANES), LANES), LANES)
        copy = pltpu.make_async_remote_copy(
            field.at[pl.ds(main + SMOOTH, tip), pl.ds(*band_of(q)), lanes],
            sides.at[j, pl.ds(main, tip), pl.ds(*band_of(q))],
            c_send.at[j], c_recv.at[j, piece(phase, q)],
            device_id={"col": lax.rem(peer + n_col, n_col)}, device_id_type=MESH,
        )
        return copy, jnp.logical_and(peer >= 0, peer < n_col)

    def raise_piece(phase, q):
        for d in range(1, n_ch):
            from_ch(d, piece_slot(phase), q, piece(phase, q)).wait_recv()
        at = (pl.ds(main, tip), pl.ds(*band_of(q)), lanes_of(phase))
        top = part[(0,) + at]
        for h in range(1, n_ch):
            top = top + part[(h,) + at]
        field[(pl.ds(main + SMOOTH, tip),) + at[1:]] = scale[at] * top
        copy, there = piece_side(phase, q, False)

        @pl.when(there)
        def _():
            copy.start()

    def finish_band(q):
        band = band_of(q)
        for phase in range(2):
            copy, there = piece_side(phase, q, True)

            @pl.when(there)
            def _():
                copy.wait_recv()

        join_rows(main, tip, band)
        for e in range(main + 2, edge + 1):
            one(e, band)
        for e in range(main + 1, edge + 2):
            two(e, band)
        for e in range(main, min(edge + 3, last)):
            three(e, band)

    widen_chunk(chunks - 2)
    sweep_chunk(chunks - 2)
    def rise(phase):
        def body(q, carry):
            raise_piece(phase, q)
            return carry
        return body

    def finish(q, carry):
        finish_band(q)
        return carry

    lax.fori_loop(0, bands, rise(0), 0)
    widen_chunk(chunks - 1)
    sweep_chunk(chunks - 1)
    lax.fori_loop(0, bands, rise(1), 0)
    lax.fori_loop(0, bands, finish, 0)
    for d in range(1, n_ch):
        whole = part.at[me_ch, pl.ds(0, early)]
        pltpu.make_async_remote_copy(
            whole, whole, t_send.at[d - 1], t_recv.at[d - 1, 0],
            device_id={"ch": lax.rem(me_ch + d, n_ch)}, device_id_type=MESH,
        ).wait_send()

    def all_field_side(step):
        j = int(step < 0)
        return beside(step, sides.at[j], sides.at[j], (c_send.at[j], c_recv.at[j, 0]))

    sent_pair(all_field_side, me_col, n_col)


def store_kernel(done, new_channel, out_hbm, nc_hbm, sem):
    copies = [pltpu.make_async_copy(new_channel, nc_hbm, sem.at[0])]
    halves, groups = done.shape[:2]
    for h in range(halves):
        for g in range(groups):
            target = out_hbm.at[:, pl.ds(g * SUB, SUB), pl.ds(h * LANES, LANES)]
            copies.append(pltpu.make_async_copy(done.at[h, g], target, sem.at[len(copies)]))
    for copy in copies:
        copy.start()
    for copy in copies:
        copy.wait()


def shards(sizes, spectra, pixel_factor, channel_factor, labels):
    n_row, n_col, n_ch = sizes
    rank, rows, cols = pixel_factor.shape
    chans = spectra.shape[0]
    share = rank // n_col
    early = rows - EARLY
    pieces = (early - SMOOTH) // CHUNK + 2 * (rank // BAND)
    news = n_col * n_ch - 1 + (n_col - 1) * (HALVES - 1)
    tall = rows + 2 * SMOOTH
    wide = cols + LANES
    halves, groups = cols // LANES, rows // SUB
    f32 = jnp.float32
    anywhere = pl.BlockSpec(memory_space=pl.ANY)
    dma = pltpu.SemaphoreType.DMA
    kept = pl.BlockSpec(memory_space=pltpu.VMEM)
    done, new_channel = pl.pallas_call(
        functools.partial(factor_kernel, sizes),
        out_shape=(
            pltpu.VMEM((halves, groups, rank, SUB, LANES), f32),
            pltpu.VMEM(channel_factor.shape, f32),
        ),
        in_specs=[anywhere] * 4,
        out_specs=(kept, kept),
        scratch_shapes=[
            pltpu.VMEM(channel_factor.shape, f32),
            pltpu.VMEM(labels.shape, labels.dtype),
            pltpu.VMEM((groups, halves, chans, SUB, LANES), f32),
            pltpu.VMEM((groups, halves, rank, SUB, LANES), f32),
            pltpu.VMEM((rows, rank + chans, cols), jnp.bfloat16),
            pltpu.VMEM((rows, rank + chans, cols), jnp.bfloat16),
            pltpu.VMEM((n_ch - 1, halves, chans, SUB, LANES), f32),
            pltpu.VMEM((rank + 2 * chans, 2 * rank), f32),
            pltpu.VMEM((n_col, share, rank + chans), f32),
            pltpu.VMEM((n_col - 1, share, rank + chans), f32),
            pltpu.VMEM((n_row, share, rank + chans), f32),
            pltpu.VMEM((n_ch, n_col, share, chans), f32),
            pltpu.VMEM((n_ch, rows, rank, cols), f32),
            pltpu.VMEM((rows, rank, cols), f32),
            pltpu.VMEM((tall, rank, wide), f32),
            pltpu.VMEM((2, rows, rank, LANES), f32),
            pltpu.VMEM((tall, SUB, wide), f32),
            pltpu.VMEM((rows, SUB, LANES), f32),
            pltpu.VMEM((rows, SUB, LANES), f32),
            pltpu.VMEM((tall, 5, SUB, wide), f32),
            pltpu.VMEM((tall, rank, wide), f32),
            pltpu.VMEM((tall, rank, wide), f32),
            dma((2, halves, groups)),
            dma((n_ch - 1, halves)), dma((n_ch - 1, halves)),
            dma((1,)), dma((n_col - 1, HALVES)),
            dma((1,)), dma((n_row - 1, HALVES)),
            dma((news,)), dma((news,)),
            dma((n_ch - 1,)), dma((n_ch - 1, pieces)),
            dma((2,)), dma((2, pieces + 1)),
            dma((2,)), dma((2,)),
            dma((4,)), dma((4,)),
            dma((2,)),
            pltpu.SemaphoreType.REGULAR((2, max(n_row - 2, 1))),
        ],
        compiler_params=pltpu.CompilerParams(
            collective_id=0, has_side_effects=True, vmem_limit_bytes=52 * 1024 * 1024
        ),
        name="factor",
    )(spectra, pixel_factor, channel_factor, labels)
    return pl.pallas_call(
        store_kernel,
        out_shape=(
            jax.ShapeDtypeStruct(pixel_factor.shape, f32),
            jax.ShapeDtypeStruct(channel_factor.shape, f32),
        ),
        in_specs=[kept, kept],
        out_specs=(anywhere, anywhere),
        scratch_shapes=[dma((halves * groups + 1,))],
        compiler_params=pltpu.CompilerParams(vmem_limit_bytes=4 * 1024 * 1024),
        name="store",
    )(done, new_channel)


def solution(mesh):
    sizes = tuple(mesh.shape[a] for a in ("row", "col", "ch"))
    placed = (P("ch", "row", "col"), P(None, "row", "col"), P(None, "ch"), P("row", "col"))
    return jax.shard_map(
        functools.partial(shards, sizes),
        mesh=mesh,
        in_specs=placed,
        out_specs=(P(None, "row", "col"), P(None, "ch")),
        check_vma=False,
    )
```
